256 devices in a mesh: ctx: 32 (over y, z), head: 8 (over x, core).
Axes of the slice: x: 4, y: 4, z: 8, core: 2. Of those that a mesh axis runs over, the one named last changes fastest.
Arguments:
- queries: bfloat16 [32768, 4096], P('ctx', 'head'), as said below
- key_value: bfloat16 [2, 32768, 4096], P(None, 'ctx', 'head'), as said below
- lanczos_vec: float32 [32768, 4096], P('ctx', 'head'), as said below
- rand_blocks: int32 [256, 3], replicated, may hold values from 0 to 255, as said below
- global_ids: int32 [2], replicated, may hold values from 0 to 255
Outputs:
- next_vec: float32 [32768, 4096], P('ctx', 'head')
- coefficients: float32 [2], replicated
The draws below stay inside these ranges and needn't reach their ends.
Inputs may be any that keep to these rules, and one draw needn't show every extreme that they name: `rand_blocks`: row b lists the random key blocks of query block b. For each shard of 8 query blocks along ctx and each shard of 8 key blocks, at most 1 of the shard's listed random blocks lie in that key shard, and every query shard reaches 1 with some key shard. `queries`: entries are of order one or a few tens. `key_value`: keys of order one, values of order one to a few hundred. `lanczos_vec`: nonzero real entries; the mean of their squares over all entries is one, up to float32 rounding.
All inputs are finite; a program needn't handle non-finite values.
Results may differ from the reference program's by a relative error of at most 0.0049.
Values may be sent and summed in bfloat16 or wider, within the bound.
No kernel may reach another device: no remote copies, remote signals or barrier semaphores. Data moves between devices by JAX's collectives and lax.ppermute only.
A program may use at most 128 MiB of HBM per device.

```python
import jax
import jax.numpy as jnp
from jax import lax

HEADS = 32
HD = 128
BS = 128
RAND = 3
GLOB = 2
QB_DEV = 8
DM = 4096
NB = 256
SEQ = 32768
N_CTX = 32


def shared_keys(key):
    base = jax.random.truncated_normal(jax.random.fold_in(key, 101), -6.0, 6.0, (SEQ, HEADS * HD), jnp.float32)
    return base


def draw_key_value(key, part):
    keys = shared_keys(key)
    block_factor = 10.0 ** jax.random.uniform(jax.random.fold_in(key, 105), (SEQ // BS,), jnp.float32, 0.0, 1.5)
    row_factor = jnp.repeat(block_factor, BS)
    values = 3.0 * jax.random.truncated_normal(jax.random.fold_in(key, 103), -6.0, 6.0, (SEQ, HEADS * HD), jnp.float32)
    values = values * row_factor[:, None]
    return jnp.stack([keys, values]).astype(jnp.bfloat16)


def draw_queries(key, part):
    base = jax.random.truncated_normal(jax.random.fold_in(key, 104), -6.0, 6.0, (SEQ, HEADS * HD), jnp.float32)
    return base.astype(jnp.bfloat16)


def draw_lanczos_vec(key, part):
    position = jnp.arange(SEQ, dtype=jnp.float32) / SEQ
    row_scale = 10.0 ** jax.random.uniform(jax.random.fold_in(key, 201), (SEQ,), jnp.float32)
    col_scale = 10.0 ** jax.random.uniform(jax.random.fold_in(key, 202), (HEADS * HD,), jnp.float32)
    noise = jax.random.truncated_normal(jax.random.fold_in(key, 204), -4.0, 4.0, (SEQ, HEADS * HD), jnp.float32)
    ramp = 3.0 ** position
    raw = noise * (ramp * row_scale)[:, None] * col_scale[None, :]
    spread = jnp.sqrt(jnp.mean(raw * raw))
    return (raw / spread).astype(jnp.float32)


def draw_rand_blocks(key, part):
    request_count = QB_DEV * RAND
    perm_keys = jax.random.split(jax.random.fold_in(key, 301), N_CTX)
    orders = jax.vmap(lambda single: jax.random.permutation(single, N_CTX))(perm_keys)
    columns = jnp.arange(request_count) % N_CTX
    sources = orders[:, columns]
    inside = jax.random.randint(jax.random.fold_in(key, 302), (N_CTX, request_count), 0, QB_DEV)
    return (sources * QB_DEV + inside).reshape(N_CTX * QB_DEV, RAND).astype(jnp.int32)


def setup_inputs(seed: int = 0) -> dict:
    seeds = jax.random.split(jax.random.key(seed), 6)
    queries = draw_queries(jax.random.fold_in(seeds[5], 71), 0)
    key_value = draw_key_value(jax.random.fold_in(seeds[5], 71), 0)
    lanczos_vec = draw_lanczos_vec(jax.random.fold_in(seeds[5], 71), 0)
    rand_blocks = draw_rand_blocks(jax.random.fold_in(seeds[5], 71), 0)
    global_ids = jax.random.randint(seeds[4], (GLOB,), 0, NB).astype(jnp.int32)
    return {"queries": queries, "key_value": key_value, "lanczos_vec": lanczos_vec, "rand_blocks": rand_blocks, "global_ids": global_ids}


def reference(queries, key_value, lanczos_vec, rand_blocks, global_ids):
    score_scale = HD ** (-0.5)
    block_ids = jnp.arange(NB, dtype=jnp.int32)
    window_part = block_ids[:, None] + jnp.arange(-1, 2, dtype=jnp.int32)[None, :]
    global_part = jnp.broadcast_to(global_ids[None, :], (NB, GLOB)).astype(jnp.int32)
    key_table = jnp.concatenate([window_part, global_part, rand_blocks.astype(jnp.int32)], axis=1)
    window_ok = (window_part >= 0) & (window_part < NB)
    valid_table = jnp.concatenate([window_ok, jnp.ones((NB, GLOB + RAND), dtype=bool)], axis=1)
    key_table = jnp.clip(key_table, 0, NB - 1).astype(jnp.int32)
    tangent_all = lanczos_vec.astype(jnp.bfloat16)

    def one_block(block):
        block_row = key_table[block]
        valid_row = valid_table[block]
        token_index = (block_row[:, None] * BS + jnp.arange(BS, dtype=jnp.int32)[None, :]).reshape(-1)
        keys = jnp.take(key_value[0], token_index, axis=0).astype(jnp.float32).reshape(-1, HEADS, HD)
        values = jnp.take(key_value[1], token_index, axis=0).astype(jnp.float32).reshape(-1, HEADS, HD)
        start = (block * BS).astype(jnp.int32)
        query = lax.dynamic_slice_in_dim(queries, start, BS, 0).astype(jnp.float32).reshape(BS, HEADS, HD)
        tangent = lax.dynamic_slice_in_dim(tangent_all, start, BS, 0).astype(jnp.float32).reshape(BS, HEADS, HD)
        valid_keys = jnp.repeat(valid_row, BS)[None, None, :]
        scores = jnp.einsum('qhd,khd->hqk', query, keys) * score_scale
        row_top = lax.optimization_barrier(jnp.max(jnp.where(valid_keys, scores, -jnp.inf), axis=-1, keepdims=True))
        weights = jnp.where(valid_keys, jnp.exp(scores - row_top), 0.0)
        attention = weights / lax.optimization_barrier(jnp.sum(weights, axis=-1, keepdims=True))
        dscore = jnp.einsum('qhd,khd->hqk', tangent, keys) * score_scale
        center = lax.optimization_barrier(jnp.sum(attention * dscore, axis=-1, keepdims=True))
        first_grad = lax.optimization_barrier((attention * (dscore - center)).astype(jnp.bfloat16)).astype(jnp.float32)
        tangent_out = jnp.einsum('hqk,khd->qhd', first_grad, values)
        tangent_out = lax.optimization_barrier(tangent_out.astype(jnp.bfloat16)).astype(jnp.float32)
        back_prob = jnp.einsum('qhd,khd->hqk', tangent_out, values)
        center_two = lax.optimization_barrier(jnp.sum(attention * back_prob, axis=-1, keepdims=True))
        second_grad = lax.optimization_barrier((attention * (back_prob - center_two)).astype(jnp.bfloat16)).astype(jnp.float32)
        image = jnp.einsum('hqk,khd->qhd', second_grad, keys) * score_scale
        return image.reshape(BS, HEADS * HD)
    product = lax.map(one_block, block_ids).reshape(SEQ, DM)
    entry_count = float(SEQ * DM)
    alpha_coef = jnp.sum(lanczos_vec * product) / entry_count
    residual = product - alpha_coef * lanczos_vec
    beta_coef = jnp.sqrt(jnp.sum(residual * residual) / entry_count + 1e-06)
    return (residual / beta_coef, jnp.stack([alpha_coef, beta_coef]))
```

```python
import functools

import jax
import jax.numpy as jnp
from jax import lax
from jax.experimental import pallas as pl
from jax.experimental.pallas import tpu as pltpu
from jax.sharding import PartitionSpec as P

HD = 128
BS = 128
LIST = 8
SCALE = HD ** (-0.5)
LOG2E = 1.4426950408889634
NT = (((1,), (1,)), ((), ()))


def attend_tile(q, tangent, keys, values, left_bias, right_bias):
    both = jnp.concatenate([q, tangent], axis=0)
    logits = lax.dot_general(both, keys, NT, preferred_element_type=jnp.float32)
    scores = logits[:BS]
    dots = logits[BS:]
    scores = jnp.concatenate(
        [
            scores[:, :BS] + left_bias,
            scores[:, BS : 2 * BS],
            scores[:, 2 * BS : 3 * BS] + right_bias,
            scores[:, 3 * BS :],
        ],
        axis=1,
    )
    row_top = jnp.max(scores, axis=1, keepdims=True)
    weights = jnp.exp2((scores - row_top) * (SCALE * LOG2E))
    inv_total = 1.0 / jnp.sum(weights, axis=1, keepdims=True)
    prob = weights * inv_total
    center = jnp.sum(prob * dots, axis=1, keepdims=True)
    first = ((prob * SCALE) * (dots - center)).astype(jnp.bfloat16)
    dout = jnp.dot(first, values, preferred_element_type=jnp.float32).astype(jnp.bfloat16)
    dprob = lax.dot_general(dout, values, NT, preferred_element_type=jnp.float32)
    center_two = jnp.sum(prob * dprob, axis=1, keepdims=True)
    second = (prob * (dprob - center_two)).astype(jnp.bfloat16)
    return jnp.dot(second, keys, preferred_element_type=jnp.float32) * SCALE


def attention_kernel(
    nblocks, rand_ref, edge_ref, q_ref, vec_ref, own, left, right, glob, rand,
    out_ref, stat_ref, kbuf, vbuf, sems, acc,
):
    b = pl.program_id(0)
    width = q_ref.shape[1]

    def copies(blk, slot, start):
        def move(src, pos):
            for kv, buf in enumerate((kbuf, vbuf)):
                cp = pltpu.make_async_copy(
                    src(kv), buf.at[slot, pl.ds(pos * BS, BS)], sems.at[slot, kv, pos]
                )
                if start:
                    cp.start()
                else:
                    cp.wait()

        if start:
            @pl.when(blk == 0)
            def _():
                move(lambda kv: left.at[kv], 0)

            @pl.when(blk > 0)
            def _():
                move(lambda kv: own.at[kv, blk - 1], 0)

            @pl.when(blk == nblocks - 1)
            def _():
                move(lambda kv: right.at[kv], 2)

            @pl.when(blk < nblocks - 1)
            def _():
                move(lambda kv: own.at[kv, blk + 1], 2)
        else:
            move(lambda kv: left.at[kv], 0)
            move(lambda kv: left.at[kv], 2)
        move(lambda kv: own.at[kv, blk], 1)
        for g in range(2):
            move(lambda kv: glob.at[kv, g], 3 + g)
        for r in range(3):
            move(lambda kv: rand.at[kv, rand_ref[blk * 3 + r]], 5 + r)

    slot = lax.rem(b, 2)

    @pl.when(b == 0)
    def _():
        copies(0, 0, True)

    @pl.when(b + 1 < nblocks)
    def _():
        copies(b + 1, 1 - slot, True)

    copies(b, slot, False)
    left_bias = jnp.where((b == 0) & (edge_ref[0] == 1), -1e30, 0.0).astype(jnp.float32)
    right_bias = jnp.where((b == nblocks - 1) & (edge_ref[1] == 1), -1e30, 0.0).astype(jnp.float32)
    for h in range(width // HD):
        cols = slice(h * HD, (h + 1) * HD)
        vec = vec_ref[:, cols]
        prod = attend_tile(
            q_ref[:, cols], vec.astype(jnp.bfloat16), kbuf[slot, :, cols], vbuf[slot, :, cols],
            left_bias, right_bias,
        )
        out_ref[:, cols] = prod
        s = jnp.sum(vec * vec, axis=0, keepdims=True)
        c = jnp.sum(vec * prod, axis=0, keepdims=True)
        a = jnp.where(s > 0, c / jnp.where(s > 0, s, 1.0), 0.0)
        d = prod - a * vec
        acc[b, 0:1, cols] = s
        acc[b, 1:2, cols] = c
        acc[b, 2:3, cols] = jnp.sum(d * d, axis=0, keepdims=True)

    @pl.when(b == nblocks - 1)
    def _():
        s, c, r = combine(acc[:, 0, :], acc[:, 1, :], acc[:, 2, :])
        lane = lax.broadcasted_iota(jnp.int32, stat_ref.shape, 1)
        stat_ref[...] = jnp.where(lane == 0, s, jnp.where(lane == 1, c, jnp.where(lane == 2, r, 0.0)))


def total(x):
    return jnp.sum(jnp.sum(x, axis=0, keepdims=True), axis=1, keepdims=True)


def combine(s, c, r):
    s_all = total(s)
    c_all = total(c)
    a = jnp.where(s > 0, c / jnp.where(s > 0, s, 1.0), 0.0)
    a_all = jnp.where(s_all > 0, c_all / jnp.where(s_all > 0, s_all, 1.0), 0.0)
    gap = a - a_all
    return s_all, c_all, total(r + (s * gap) * gap)


def finish_kernel(count, gathered, prod_ref, vec_ref, out_ref, coef_ref, ab):
    @pl.when(pl.program_id(0) == 0)
    def _():
        table = gathered[...]
        s, c, r = table[:, 0:1], table[:, 1:2], table[:, 2:3]
        alpha = total(c) * (1.0 / count)
        slope = jnp.where(s > 0, c / jnp.where(s > 0, s, 1.0), 0.0)
        gap = slope - alpha
        square = total(r + (s * gap) * gap)
        beta = jnp.sqrt(square * (1.0 / count) + 1e-06)
        ab[0:1, :] = jnp.broadcast_to(alpha, (1, 128))
        ab[1:2, :] = jnp.broadcast_to(1.0 / beta, (1, 128))
        lane = lax.broadcasted_iota(jnp.int32, coef_ref.shape, 1)
        coef_ref[...] = jnp.where(lane == 0, alpha, beta)

    alpha = ab[0:1, 0:1]
    inv = ab[1:2, 0:1]
    out_ref[...] = (prod_ref[...] - alpha * vec_ref[...]) * inv


def from_root(block, axis, holder):
    block = jnp.where(lax.axis_index(axis) == holder, block, jnp.zeros_like(block))
    return lax.psum(block, axis)


def local(queries, key_value, lanczos_vec, rand_blocks, global_ids):
    rows, width = queries.shape
    nblocks = rows // BS
    nctx = lax.axis_size("ctx")
    nhead = lax.axis_size("head")
    me = lax.axis_index("ctx")
    own = key_value.reshape(2, nblocks, BS, width)
    left = lax.ppermute(own[:, nblocks - 1], "ctx", [(i, i + 1) for i in range(nctx - 1)])
    right = lax.ppermute(own[:, 0], "ctx", [(i + 1, i) for i in range(nctx - 1)])
    glob = jnp.stack(
        [
            from_root(
                lax.dynamic_index_in_dim(own, global_ids[g] % nblocks, 1, keepdims=False),
                "ctx", global_ids[g] // nblocks,
            )
            for g in range(2)
        ],
        axis=1,
    )
    requests = rand_blocks.reshape(nctx, nblocks * 3)
    mine = requests // nblocks == me
    chosen = jnp.sum(jnp.where(mine, requests % nblocks, 0), axis=1)
    outgoing = jnp.take(own, chosen, axis=1)
    incoming = lax.all_to_all(outgoing, "ctx", split_axis=1, concat_axis=1, tiled=True)
    rand_slots = lax.dynamic_index_in_dim(requests, me, 0, keepdims=False) // nblocks
    edges = jnp.stack([(me == 0).astype(jnp.int32), (me == nctx - 1).astype(jnp.int32)])
    any_spec = pl.BlockSpec(memory_space=pl.ANY)
    row_spec = pl.BlockSpec((BS, width), lambda b, *_: (b, 0))
    product, stats = pl.pallas_call(
        functools.partial(attention_kernel, nblocks),
        out_shape=(
            jax.ShapeDtypeStruct((rows, width), jnp.float32),
            jax.ShapeDtypeStruct((8, 128), jnp.float32),
        ),
        grid_spec=pltpu.PrefetchScalarGridSpec(
            num_scalar_prefetch=2,
            grid=(nblocks,),
            in_specs=[row_spec, row_spec] + [any_spec] * 5,
            out_specs=(row_spec, pl.BlockSpec((8, 128), lambda b, *_: (0, 0))),
            scratch_shapes=[
                pltpu.VMEM((2, LIST * BS, width), jnp.bfloat16),
                pltpu.VMEM((2, LIST * BS, width), jnp.bfloat16),
                pltpu.SemaphoreType.DMA((2, 2, LIST)),
                pltpu.VMEM((nblocks, 8, width), jnp.float32),
            ],
        ),
        name="attend",
    )(rand_slots, edges, queries, lanczos_vec, own, left, right, glob, incoming)
    sent = jnp.broadcast_to(stats[:1], (nctx * nhead, 128))
    gathered = lax.all_to_all(sent, ("ctx", "head"), 0, 0, tiled=True)
    count = float(rows * width * nctx * nhead)
    step = rows // 4
    fin_spec = pl.BlockSpec((step, width), lambda i: (i, 0))
    next_vec, coef = pl.pallas_call(
        functools.partial(finish_kernel, count),
        out_shape=(
            jax.ShapeDtypeStruct((rows, width), jnp.float32),
            jax.ShapeDtypeStruct((8, 128), jnp.float32),
        ),
        grid=(4,),
        in_specs=[pl.BlockSpec((nctx * nhead, 128), lambda i: (0, 0)), fin_spec, fin_spec],
        out_specs=(fin_spec, pl.BlockSpec((8, 128), lambda i: (0, 0))),
        scratch_shapes=[pltpu.VMEM((8, 128), jnp.float32)],
        name="finish",
    )(gathered, product, lanczos_vec)
    return next_vec, coef[0, :2]


def solution(mesh):
    placed = (P("ctx", "head"), P(None, "ctx", "head"), P("ctx", "head"), P(), P())
    return jax.shard_map(
        local, mesh=mesh, in_specs=placed, out_specs=(P("ctx", "head"), P()), check_vma=False
    )
```

```python
import functools

import jax
import jax.numpy as jnp
from jax import lax
from jax.experimental import pallas as pl
from jax.experimental.pallas import tpu as pltpu
from jax.sharding import PartitionSpec as P

HD = 128
BS = 128
LIST = 8
SCALE = HD ** (-0.5)
LOG2E = 1.4426950408889634
NT = (((1,), (1,)), ((), ()))


def attend_tile(q, tangent, keys, values, left_bias, right_bias):
    both = jnp.concatenate([q, tangent], axis=0)
    logits = lax.dot_general(both, keys, NT, preferred_element_type=jnp.float32)
    scores = logits[:BS]
    dots = logits[BS:]
    scores = jnp.concatenate(
        [
            scores[:, :BS] + left_bias,
            scores[:, BS : 2 * BS],
            scores[:, 2 * BS : 3 * BS] + right_bias,
            scores[:, 3 * BS :],
        ],
        axis=1,
    )
    row_top = jnp.max(scores, axis=1, keepdims=True)
    weights = jnp.exp2((scores - row_top) * (SCALE * LOG2E))
    inv_total = 1.0 / jnp.sum(weights, axis=1, keepdims=True)
    prob = weights * inv_total
    center = jnp.sum(prob * dots, axis=1, keepdims=True)
    first = ((prob * SCALE) * (dots - center)).astype(jnp.bfloat16)
    dout = jnp.dot(first, values, preferred_element_type=jnp.float32).astype(jnp.bfloat16)
    dprob = lax.dot_general(dout, values, NT, preferred_element_type=jnp.float32)
    center_two = jnp.sum(prob * dprob, axis=1, keepdims=True)
    second = (prob * (dprob - center_two)).astype(jnp.bfloat16)
    return jnp.dot(second, keys, preferred_element_type=jnp.float32) * SCALE


NY, NZ = 4, 8
CHUNKS = ((0, 2), (2, 1), (3, 1))
OWN, L1, L2, A3, A4, B3, R2, R1, YP, YM, Y2, LYP, LYM, LY2, LOC = range(15)


def start_choice(arrays, ids, code, dst, sem):
    which = lax.shift_right_logical(code, 3)
    slot = code & 7
    for k in ids:
        @pl.when(which == k)
        def _(k=k):
            pltpu.make_async_copy(arrays[k].at[slot], dst, sem).start()


def attention_kernel(nblocks, chunk, code_ref, q_ref, vec_ref, *refs):
    arrays = refs[:15]
    out_ref, stat_ref, kvbuf, sems, acc = refs[15:]
    b = pl.program_id(0)
    width = q_ref.shape[1]

    def place(slot, pos):
        return kvbuf.at[slot, :, pl.ds(pos * BS, BS)]

    def start(blk, slot):
        for pos in range(LIST):
            ids = (
                (OWN, L1, YP) if pos == 0 else (OWN,) if pos == 1 else (OWN, R1, YM) if pos == 2
                else (LYP, LYM, LY2, LOC) if pos < 5 else tuple(range(LOC))
            )
            start_choice(arrays, ids, code_ref[blk * LIST + pos], place(slot, pos), sems.at[slot, pos])

    slot = lax.rem(b, 2)

    @pl.when(b == 0)
    def _():
        start(0, 0)

    @pl.when(b + 1 < nblocks)
    def _():
        start(b + 1, 1 - slot)

    for pos in range(LIST):
        pltpu.make_async_copy(arrays[OWN].at[0], place(slot, pos), sems.at[slot, pos]).wait()
    edge = nblocks * LIST
    left_bias = jnp.where((b == 0) & (code_ref[edge] == 1), -1e30, 0.0).astype(jnp.float32)
    right_bias = jnp.where((b == nblocks - 1) & (code_ref[edge + 1] == 1), -1e30, 0.0).astype(jnp.float32)
    for h in range(width // HD):
        cols = slice(h * HD, (h + 1) * HD)
        vec = vec_ref[:, cols]
        prod = attend_tile(
            q_ref[:, cols], vec.astype(jnp.bfloat16), kvbuf[slot, 0, :, cols], kvbuf[slot, 1, :, cols],
            left_bias, right_bias,
        )
        out_ref[:, cols] = prod
        s = jnp.sum(vec * vec, axis=0, keepdims=True)
        c = jnp.sum(vec * prod, axis=0, keepdims=True)
        a = jnp.where(s > 0, c / jnp.where(s > 0, s, 1.0), 0.0)
        d = prod - a * vec
        acc[b, 0:1, cols] = s
        acc[b, 1:2, cols] = c
        acc[b, 2:3, cols] = jnp.sum(d * d, axis=0, keepdims=True)

    @pl.when(b == nblocks - 1)
    def _():
        s, c, r = combine(acc[:, 0, :], acc[:, 1, :], acc[:, 2, :])
        lane = lax.broadcasted_iota(jnp.int32, stat_ref.shape, 1) - 3 * chunk
        stat_ref[...] = jnp.where(lane == 0, s, jnp.where(lane == 1, c, jnp.where(lane == 2, r, 0.0)))


def run_copies(plan, sems):
    copies = [pltpu.make_async_copy(src, dst, sems.at[i]) for i, (src, dst) in enumerate(plan)]
    for cp in copies:
        cp.start()
    for cp in copies:
        cp.wait()


def third_hop_kernel(pick_ref, l2, r2, plus, minus, sems):
    run_copies(
        [(l2.at[pick_ref[i]], plus.at[i]) for i in range(8)]
        + [(r2.at[pick_ref[8 + i]], minus.at[i]) for i in range(8)],
        sems,
    )


def early_rows_kernel(pick_ref, own, l1, r1, l2, r2, yp, y2, ym, sems):
    plan = []
    for row, out in enumerate((yp, y2, ym)):
        for i, src in enumerate((own, l1, r1, l2, r2)):
            plan.append((src.at[pick_ref[16 + row * 5 + i]], out.at[i]))
    plan.append((l1.at[7], yp.at[5]))
    plan.append((r1.at[0], ym.at[5]))
    run_copies(plan, sems)


def late_rows_kernel(pick_ref, own, l1, r1, l2, r2, a3, b3, a4, b4, yp, y2, ym, sems):
    arrays = {OWN: own, L1: l1, L2: l2, A3: a3, A4: a4, B3: b3, R2: r2, R1: r1, 8: b4}
    outs = (yp, y2, ym)
    for g in range(2):
        for row, out in enumerate(outs):
            start_choice(arrays, range(9), pick_ref[31 + g], out.at[3 + g], sems.at[9 + g * 3 + row])
    last = (a4.at[1], b4.at[0], b4.at[1])
    plan = []
    for row, out in enumerate(outs):
        plan += [(a3.at[row + 1], out.at[0]), (b3.at[row + 1], out.at[1]), (last[row], out.at[2])]
    run_copies(plan, sems)
    for g in range(2):
        for row, out in enumerate(outs):
            pltpu.make_async_copy(own.at[0], out.at[3 + g], sems.at[9 + g * 3 + row]).wait()


def total(x):
    return jnp.sum(jnp.sum(x, axis=0, keepdims=True), axis=1, keepdims=True)


def combine(s, c, r):
    s_all = total(s)
    c_all = total(c)
    a = jnp.where(s > 0, c / jnp.where(s > 0, s, 1.0), 0.0)
    a_all = jnp.where(s_all > 0, c_all / jnp.where(s_all > 0, s_all, 1.0), 0.0)
    gap = a - a_all
    return s_all, c_all, total(r + (s * gap) * gap)


def finish_kernel(count, gathered, *refs):
    prods = refs[: len(CHUNKS)]
    vec_ref, out_ref, coef_ref, ab = refs[len(CHUNKS) :]

    @pl.when(pl.program_id(0) == 0)
    def _():
        table = gathered[...]
        parts = [[table[:, 3 * k + i : 3 * k + i + 1] for i in range(3)] for k in range(len(CHUNKS))]
        alpha = sum(total(c) for _, c, _ in parts) * (1.0 / count)
        square = 0.0
        for s, c, r in parts:
            gap = jnp.where(s > 0, c / jnp.where(s > 0, s, 1.0), 0.0) - alpha
            square = square + total(r + (s * gap) * gap)
        beta = jnp.sqrt(square * (1.0 / count) + 1e-06)
        ab[0:1, :] = jnp.broadcast_to(alpha, (1, 128))
        ab[1:2, :] = jnp.broadcast_to(1.0 / beta, (1, 128))
        lane = lax.broadcasted_iota(jnp.int32, coef_ref.shape, 1)
        coef_ref[...] = jnp.where(lane == 0, alpha, beta)

    alpha = ab[0:1, 0:1]
    inv = ab[1:2, 0:1]
    for (first, heads), prod in zip(CHUNKS, prods):
        cols = slice(first * HD, (first + heads) * HD)
        out_ref[:, cols] = (prod[...] - alpha * vec_ref[:, cols]) * inv


def z_shift(d):
    return [(y * NZ + z, y * NZ + (z + d) % NZ) for y in range(NY) for z in range(NZ)]


def y_shift(d):
    return [(y * NZ + z, (y + d) % NY * NZ + z) for y in range(NY) for z in range(NZ)]


def send(name, x, pairs):
    with jax.named_scope(name):
        return lax.ppermute(x, "ctx", pairs)


ANY = pl.BlockSpec(memory_space=pl.ANY)


def pack(kernel, name, picks, arrays, counts, ncopies):
    shape = arrays[0].shape[1:]
    return pl.pallas_call(
        kernel,
        out_shape=tuple(jax.ShapeDtypeStruct((n,) + shape, jnp.bfloat16) for n in counts),
        grid_spec=pltpu.PrefetchScalarGridSpec(
            num_scalar_prefetch=1,
            grid=(),
            in_specs=[ANY] * len(arrays),
            out_specs=tuple(pl.BlockSpec(memory_space=pltpu.VMEM) for _ in counts),
            scratch_shapes=[pltpu.SemaphoreType.DMA((ncopies,))],
        ),
        name=name,
    )(picks, *arrays)


def tables(rand_blocks, global_ids, me, nblocks, nctx):
    my_y, my_z = me // NZ, me % NZ
    requests = rand_blocks.reshape(nctx, nblocks * 3)
    mine = lax.dynamic_index_in_dim(requests, me, 0, keepdims=False)
    pairs = []
    for i in range(4):
        pairs.append((i, 1, 0, -2))
    pairs += [(0, 2, 0, -2), (1, 2, 0, -2), None, None]
    for i in range(4):
        pairs.append((i, -1, 0, 2))
    pairs += [(2, -2, 0, 2), (3, -2, 0, 2), None, None]
    for row in (1, 2, 3):
        pairs += [(row, 0, 0, d) for d in (0, -1, 1, -2, 2)]
    filled = [p if p is not None else (0, 0, 0, 0) for p in pairs]
    grid = jnp.array(filled, jnp.int32)
    consumer = (my_y + grid[:, 0]) % NY * NZ + (my_z + grid[:, 1]) % NZ
    source = my_y * NZ + (my_z + grid[:, 3]) % NZ
    wanted = requests[consumer]
    picks = jnp.sum(jnp.where(wanted // nblocks == source[:, None], wanted % nblocks, 0), axis=1)
    g_in = global_ids % nblocks
    g_z = global_ids // nblocks % NZ
    g_y = global_ids // nblocks // NZ
    place = jnp.arange(len(pairs))
    g0_places = (place == 6) | (place == 15)
    g1_places = (place == 7) | (place == 14)
    picks = jnp.where(g0_places, g_in[0], jnp.where(g1_places, g_in[1], picks))
    far = (my_z - g_z) % NZ
    g_slot = jnp.where(
        far == 3, jnp.array([6, 7]), jnp.where(far == 5, jnp.array([7, 6]), jnp.where(far == 4, 2, g_in))
    )
    g_arr = jnp.where(far == 4, jnp.array([A4, 8]), far)
    picks = jnp.concatenate([picks, g_arr * 8 + g_slot]).astype(jnp.int32)
    src = mine // nblocks
    inside = mine % nblocks
    dy = (src // NZ - my_y) % NY
    dz = (my_z - src % NZ) % NZ
    late = (dz >= 3) & (dz <= 5)
    near_slot = jnp.where(dz == 3, 0, jnp.where(dz == 5, 0, jnp.where(dz == 4, 0, inside)))
    far_slot = jnp.where(
        late, jnp.where(dz == 3, 0, jnp.where(dz == 5, 1, 2)),
        jnp.where(dz == 0, 0, jnp.where(dz == 1, 1, jnp.where(dz == 7, 2, jnp.where(dz == 2, 3, 4)))),
    )
    row_arr = jnp.where(dy == 1, YM, jnp.where(dy == 2, Y2, YP)) + jnp.where(late, LYP - YP, 0)
    rand_code = jnp.where(dy == 0, dz * 8 + near_slot, row_arr * 8 + far_slot).reshape(nblocks, 3)
    gy = (g_y - my_y) % NY
    g_list = jnp.where(gy == 0, LOC, jnp.where(gy == 1, LYM, jnp.where(gy == 2, LY2, LYP))) * 8 + 3 + jnp.arange(2)
    block = jnp.arange(nblocks)
    left = jnp.where(block == 0, jnp.where(my_z == 0, YP * 8 + 5, L1 * 8 + nblocks - 1), block - 1)
    right = jnp.where(block == nblocks - 1, jnp.where(my_z == NZ - 1, YM * 8 + 5, R1 * 8), block + 1)
    codes = jnp.concatenate(
        [jnp.stack([left, block, right], axis=1), jnp.broadcast_to(g_list, (nblocks, 2)), rand_code], axis=1
    ).reshape(-1)
    edges = jnp.stack([me == 0, me == nctx - 1]).astype(jnp.int32)
    return picks, jnp.concatenate([codes.astype(jnp.int32), edges])


def local(queries, key_value, lanczos_vec, rand_blocks, global_ids):
    rows, width = queries.shape
    nblocks = rows // BS
    nctx = lax.axis_size("ctx")
    nhead = lax.axis_size("head")
    me = lax.axis_index("ctx")
    picks, codes = tables(rand_blocks, global_ids, me, nblocks, nctx)
    blocks = key_value.reshape(2, nblocks, BS, width)
    products = []
    stats = []
    for k, (first, heads) in enumerate(CHUNKS):
        cw = heads * HD
        own = jnp.swapaxes(blocks[..., first * HD : first * HD + cw], 0, 1)
        n = "c%d" % k
        l1 = send(n + "p1", own, z_shift(1))
        r1 = send(n + "m1", own, z_shift(-1))
        l2 = send(n + "p2", l1, z_shift(1))
        r2 = send(n + "m2", r1, z_shift(-1))
        plus, minus = pack(third_hop_kernel, n + "hop3", picks, (l2, r2), (8, 8), 16)
        a3 = send(n + "p3", plus, z_shift(1))
        b3 = send(n + "m3", minus, z_shift(-1))
        a4 = send(n + "p4", a3[4:7], z_shift(1))
        b4 = send(n + "m4", b3[4:7], z_shift(-1))
        near = (own, l1, r1, l2, r2)
        ep, e2, em = pack(early_rows_kernel, n + "early", picks, near, (6, 5, 6), 17)
        yp = send(n + "ey1", ep, y_shift(1))
        y2 = send(n + "ey2", e2, y_shift(2))
        ym = send(n + "ey3", em, y_shift(-1))
        fp, f2, fm = pack(late_rows_kernel, n + "late", picks, near + (a3, b3, a4, b4), (5, 5, 5), 15)
        lyp = send(n + "ly1", fp, y_shift(1))
        ly2 = send(n + "ly2", f2, y_shift(2))
        lym = send(n + "ly3", fm, y_shift(-1))
        arrays = (own, l1, l2, a3, a4, b3, r2, r1, yp, ym, y2, lyp, lym, ly2, fp)
        col_spec = pl.BlockSpec((BS, cw), lambda b, *_, at=first // heads: (b, at))
        out_spec = pl.BlockSpec((BS, cw), lambda b, *_: (b, 0))
        keys = LIST * BS
        product, stat = pl.pallas_call(
            functools.partial(attention_kernel, nblocks, k),
            out_shape=(
                jax.ShapeDtypeStruct((rows, cw), jnp.float32),
                jax.ShapeDtypeStruct((8, 128), jnp.float32),
            ),
            grid_spec=pltpu.PrefetchScalarGridSpec(
                num_scalar_prefetch=1,
                grid=(nblocks,),
                in_specs=[col_spec, col_spec] + [ANY] * len(arrays),
                out_specs=(out_spec, pl.BlockSpec((8, 128), lambda b, *_: (0, 0))),
                scratch_shapes=[
                    pltpu.VMEM((2, 2, keys, cw), jnp.bfloat16),
                    pltpu.SemaphoreType.DMA((2, LIST)),
                    pltpu.VMEM((nblocks, 8, cw), jnp.float32),
                ],
            ),
            cost_estimate=pl.CostEstimate(
                flops=10 * rows * keys * cw, bytes_accessed=16 * rows * cw,
                transcendentals=rows * keys * heads,
            ),
            name=n + "attend",
        )(codes, queries, lanczos_vec, *arrays)
        products.append(product)
        stats.append(stat)
    sent = jnp.broadcast_to(sum(stats)[:1], (nctx * nhead, 128))
    gathered = lax.all_to_all(sent, ("ctx", "head"), 0, 0, tiled=True)
    count = float(rows * width * nctx * nhead)
    step = rows // 4
    fin_spec = pl.BlockSpec((step, width), lambda i: (i, 0))
    part_specs = [pl.BlockSpec((step, heads * HD), lambda i: (i, 0)) for _, heads in CHUNKS]
    next_vec, coef = pl.pallas_call(
        functools.partial(finish_kernel, count),
        out_shape=(
            jax.ShapeDtypeStruct((rows, width), jnp.float32),
            jax.ShapeDtypeStruct((8, 128), jnp.float32),
        ),
        grid=(4,),
        in_specs=[pl.BlockSpec((nctx * nhead, 128), lambda i: (0, 0))] + part_specs + [fin_spec],
        out_specs=(fin_spec, pl.BlockSpec((8, 128), lambda i: (0, 0))),
        scratch_shapes=[pltpu.VMEM((8, 128), jnp.float32)],
        name="finish",
    )(gathered, *products, lanczos_vec)
    return next_vec, coef[0, :2]


def solution(mesh):
    placed = (P("ctx", "head"), P(None, "ctx", "head"), P("ctx", "head"), P(), P())
    return jax.shard_map(
        local, mesh=mesh, in_specs=placed, out_specs=(P("ctx", "head"), P()), check_vma=False
    )
```

```python
import functools

import jax
import jax.numpy as jnp
from jax import lax
from jax.experimental import pallas as pl
from jax.experimental.pallas import tpu as pltpu
from jax.sharding import PartitionSpec as P


HD = 128
BS = 128
LIST = 8
SCALE = HD ** (-0.5)
LOG2E = 1.4426950408889634
NT = (((1,), (1,)), ((), ()))


def attend_tile(q, tangent, keys, values, left_bias, right_bias):
    both = jnp.concatenate([q, tangent], axis=0)
    logits = lax.dot_general(both, keys, NT, preferred_element_type=jnp.float32)
    scores = logits[:BS]
    dots = logits[BS:]
    scores = jnp.concatenate(
        [
            scores[:, :BS] + left_bias,
            scores[:, BS : 2 * BS],
            scores[:, 2 * BS : 3 * BS] + right_bias,
            scores[:, 3 * BS :],
        ],
        axis=1,
    )
    row_top = jnp.max(scores, axis=1, keepdims=True)
    weights = jnp.exp2((scores - row_top) * (SCALE * LOG2E))
    inv_total = 1.0 / jnp.sum(weights, axis=1, keepdims=True)
    prob = weights * inv_total
    center = jnp.sum(prob * dots, axis=1, keepdims=True)
    first = ((prob * SCALE) * (dots - center)).astype(jnp.bfloat16)
    dout = jnp.dot(first, values, preferred_element_type=jnp.float32).astype(jnp.bfloat16)
    dprob = lax.dot_general(dout, values, NT, preferred_element_type=jnp.float32)
    center_two = jnp.sum(prob * dprob, axis=1, keepdims=True)
    second = (prob * (dprob - center_two)).astype(jnp.bfloat16)
    return jnp.dot(second, keys, preferred_element_type=jnp.float32) * SCALE


NY, NZ = 4, 8
CHUNKS = ((0, 2), (2, 1), (3, 1))
SPLIT = (2, 1, 1)
CALLS = sum(SPLIT)
OWN, L1, _, _, _, _, _, R1, YP, YM, Y2, LYP, _, _ = range(14)


def start_choice(arrays, ids, code, dst, sem):
    which = lax.shift_right_logical(code, 3)
    slot = code & 7
    for k in ids:
        @pl.when(which == k)
        def _(k=k):
            pltpu.make_async_copy(arrays[k].at[slot], dst, sem).start()


def attention_kernel(nblocks, chunk, first_block, code_ref, q_ref, vec_ref, *refs):
    arrays = refs[:14]
    pieces = refs[14:18]
    out_ref, stat_ref, kvbuf, sems, acc = refs[18:]
    step = pl.program_id(0)
    nsteps = pl.num_programs(0)
    b = step + first_block
    width = q_ref.shape[1]
    table = nblocks * 6
    listed = (0, 1, 2, 5, 6, 7)

    def place(slot, pos):
        return kvbuf.at[slot, :, pl.ds(pos * BS, BS)]

    def globals_in(slot):
        copies = []
        cols = pl.ds(chunk[0] * HD, width)
        for i in range(NY):
            rows = pl.multiple_of(code_ref[table + 2 + i], BS // NY)
            for g in range(2):
                dst = kvbuf.at[slot, :, pl.ds((3 + g) * BS + rows, BS // NY)]
                sem = sems.at[slot, LIST + 2 * i + g]
                copies.append(pltpu.make_async_copy(pieces[i].at[g, :, :, cols], dst, sem))
        return copies

    def start(blk, slot):
        for j, pos in enumerate(listed):
            ids = (
                (OWN, L1, YP) if pos == 0 else (OWN,) if pos == 1 else (OWN, R1, YM) if pos == 2
                else tuple(range(14))
            )
            start_choice(arrays, ids, code_ref[blk * 6 + j], place(slot, pos), sems.at[slot, pos])

        @pl.when(blk < first_block + 2)
        def _():
            for cp in globals_in(slot):
                cp.start()

    slot = lax.rem(step, 2)

    @pl.when(step == 0)
    def _():
        start(b, 0)

    @pl.when(step + 1 < nsteps)
    def _():
        start(b + 1, 1 - slot)

    for pos in listed:
        pltpu.make_async_copy(arrays[OWN].at[0], place(slot, pos), sems.at[slot, pos]).wait()

    @pl.when(step < 2)
    def _():
        for cp in globals_in(slot):
            cp.wait()

    left_bias = jnp.where((b == 0) & (code_ref[table] == 1), -1e30, 0.0).astype(jnp.float32)
    right_bias = jnp.where((b == nblocks - 1) & (code_ref[table + 1] == 1), -1e30, 0.0).astype(jnp.float32)
    for h in range(width // HD):
        cols = slice(h * HD, (h + 1) * HD)
        vec = vec_ref[:, cols]
        prod = attend_tile(
            q_ref[:, cols], vec.astype(jnp.bfloat16), kvbuf[slot, 0, :, cols], kvbuf[slot, 1, :, cols],
            left_bias, right_bias,
        )
        out_ref[:, cols] = prod
        s = jnp.sum(vec * vec, axis=0, keepdims=True)
        c = jnp.sum(vec * prod, axis=0, keepdims=True)
        a = jnp.where(s > 0, c / jnp.where(s > 0, s, 1.0), 0.0)
        d = prod - a * vec
        acc[step, 0:1, cols] = s
        acc[step, 1:2, cols] = c
        acc[step, 2:3, cols] = jnp.sum(d * d, axis=0, keepdims=True)

    @pl.when(step == nsteps - 1)
    def _():
        s, c, r = combine(acc[:, 0, :], acc[:, 1, :], acc[:, 2, :])
        lane = lax.broadcasted_iota(jnp.int32, stat_ref.shape, 1) - 3 * chunk[1]
        stat_ref[...] = jnp.where(lane == 0, s, jnp.where(lane == 1, c, jnp.where(lane == 2, r, 0.0)))


def run_copies(plan, sems):
    copies = [pltpu.make_async_copy(src, dst, sems.at[i]) for i, (src, dst) in enumerate(plan)]
    for cp in copies:
        cp.start()
    for cp in copies:
        cp.wait()


def near_kernel(pick_ref, own, l1, r1, l2, r2, plus, minus, yp, y2, ym, sems):
    plan = []
    for i in range(6):
        plan.append((l2.at[pick_ref[i]], plus.at[i]))
        plan.append((r2.at[pick_ref[6 + i]], minus.at[i]))
    for row, out in enumerate((yp, y2, ym)):
        for i, src in enumerate((own, l1, r1, l2, r2)):
            plan.append((src.at[pick_ref[12 + row * 5 + i]], out.at[i]))
    plan.append((l1.at[l1.shape[0] - 1], yp.at[5]))
    plan.append((r1.at[0], ym.at[5]))
    run_copies(plan, sems)


def late_kernel(pick_ref, a3, b3, a4, b4, yp, y2, ym, sems):
    last = (a4.at[1], b4.at[0], b4.at[1])
    plan = []
    for row, out in enumerate((yp, y2, ym)):
        plan += [(a3.at[row + 1], out.at[0]), (b3.at[row + 1], out.at[1]), (last[row], out.at[2])]
    run_copies(plan, sems)


def split_kernel(pick_ref, blocks, p0, p1, p2, p3, sems):
    plan = []
    for i, out in enumerate((p0, p1, p2, p3)):
        rows = pl.ds(pl.multiple_of(pick_ref[29 + i], BS // NY), BS // NY)
        for g in range(2):
            plan.append((blocks.at[:, pick_ref[27 + g], rows], out.at[g]))
    run_copies(plan, sems)


def choose_kernel(at, pick_ref, *refs):
    srcs, out, sems = refs[:-2], refs[-2], refs[-1]
    for g in range(2):
        for k, src in enumerate(srcs):
            @pl.when(pick_ref[at + g] == k)
            def _(src=src, g=g):
                pltpu.make_async_copy(src.at[g], out.at[g], sems.at[g]).start()
    for g in range(2):
        pltpu.make_async_copy(srcs[0].at[g], out.at[g], sems.at[g]).wait()


def total(x):
    return jnp.sum(jnp.sum(x, axis=0, keepdims=True), axis=1, keepdims=True)


def combine(s, c, r):
    s_all = total(s)
    c_all = total(c)
    a = jnp.where(s > 0, c / jnp.where(s > 0, s, 1.0), 0.0)
    a_all = jnp.where(s_all > 0, c_all / jnp.where(s_all > 0, s_all, 1.0), 0.0)
    gap = a - a_all
    return s_all, c_all, total(r + (s * gap) * gap)


def finish_kernel(count, gathered, *refs):
    prods = refs[:CALLS]
    vec_ref, out_ref, coef_ref, ab = refs[CALLS:]
    step = pl.program_id(0)

    @pl.when(step == 0)
    def _():
        table = gathered[...]
        parts = [[table[:, 3 * k + i : 3 * k + i + 1] for i in range(3)] for k in range(CALLS)]
        alpha = sum(total(c) for _, c, _ in parts) * (1.0 / count)
        square = 0.0
        for s, c, r in parts:
            gap = jnp.where(s > 0, c / jnp.where(s > 0, s, 1.0), 0.0) - alpha
            square = square + total(r + (s * gap) * gap)
        beta = jnp.sqrt(square * (1.0 / count) + 1e-06)
        ab[0:1, :] = jnp.broadcast_to(alpha, (1, 128))
        ab[1:2, :] = jnp.broadcast_to(1.0 / beta, (1, 128))
        lane = lax.broadcasted_iota(jnp.int32, coef_ref.shape, 1)
        coef_ref[...] = jnp.where(lane == 0, alpha, beta)

    alpha = ab[0:1, 0:1]
    inv = ab[1:2, 0:1]
    at = 0
    for (first, heads), parts in zip(CHUNKS, SPLIT):
        cols = slice(first * HD, (first + heads) * HD)
        for part in range(parts):
            mine = step * parts // pl.num_programs(0) == part

            @pl.when(mine)
            def _(prod=prods[at], cols=cols):
                out_ref[:, cols] = (prod[...] - alpha * vec_ref[:, cols]) * inv

            at += 1


def z_shift(d):
    return [(y * NZ + z, y * NZ + (z + d) % NZ) for y in range(NY) for z in range(NZ)]


def y_shift(d):
    return [(y * NZ + z, (y + d) % NY * NZ + z) for y in range(NY) for z in range(NZ)]


def send(x, pairs):
    return lax.ppermute(x, "ctx", pairs)


ANY = pl.BlockSpec(memory_space=pltpu.HBM)


def pack(kernel, picks, arrays, shapes, ncopies):
    return pl.pallas_call(
        kernel,
        out_shape=tuple(jax.ShapeDtypeStruct(shape, jnp.bfloat16) for shape in shapes),
        grid_spec=pltpu.PrefetchScalarGridSpec(
            num_scalar_prefetch=1,
            grid=(),
            in_specs=[ANY] * len(arrays),
            out_specs=tuple(pl.BlockSpec(memory_space=pltpu.VMEM) for _ in shapes),
            scratch_shapes=[pltpu.SemaphoreType.DMA((ncopies,))],
        ),
        cost_estimate=pl.CostEstimate(flops=0, bytes_accessed=6000000, transcendentals=0),
    )(picks, *arrays)


def tables(rand_blocks, global_ids, me, nblocks, nctx):
    my_y, my_z = me // NZ, me % NZ
    requests = rand_blocks.reshape(nctx, nblocks * 3)
    mine = lax.dynamic_index_in_dim(requests, me, 0, keepdims=False)
    pairs = [(i, 1, -2) for i in range(4)] + [(0, 2, -2), (1, 2, -2)]
    pairs += [(i, -1, 2) for i in range(4)] + [(2, -2, 2), (3, -2, 2)]
    for row in (1, 2, 3):
        pairs += [(row, 0, d) for d in (0, -1, 1, -2, 2)]
    offsets = jnp.array(pairs, jnp.int32)
    consumer = ((my_y + offsets[:, 0]) & (NY - 1)) * NZ + ((my_z + offsets[:, 1]) & (NZ - 1))
    source = my_y * NZ + ((my_z + offsets[:, 2]) & (NZ - 1))
    shift = nblocks.bit_length() - 1
    wanted = requests[consumer]
    picks = jnp.sum(
        jnp.where((wanted >> shift) == source[:, None], wanted & (nblocks - 1), 0), axis=1
    )
    g_shard = global_ids >> shift
    g_y, g_z = g_shard >> 3, g_shard & (NZ - 1)
    arange4 = jnp.arange(NY)
    picks = jnp.concatenate(
        [
            picks,
            global_ids & (nblocks - 1),
            ((my_y + arange4) & (NY - 1)) * (BS // NY),
            (my_y - g_y) & (NY - 1),
            (my_z - g_z) & (NZ - 1),
        ]
    ).astype(jnp.int32)
    src = mine >> shift
    inside = mine & (nblocks - 1)
    dy = ((src >> 3) - my_y) & (NY - 1)
    dz = (my_z - src) & (NZ - 1)
    late = (dz >= 3) & (dz <= 5)
    near_slot = jnp.where(late, 0, inside)
    far_slot = jnp.where(
        late, jnp.where(dz == 3, 0, jnp.where(dz == 5, 1, 2)),
        jnp.where(dz == 0, 0, jnp.where(dz == 1, 1, jnp.where(dz == 7, 2, jnp.where(dz == 2, 3, 4)))),
    )
    row_arr = jnp.where(dy == 1, YM, jnp.where(dy == 2, Y2, YP)) + jnp.where(late, LYP - YP, 0)
    rand_code = jnp.where(dy == 0, dz * 8 + near_slot, row_arr * 8 + far_slot).reshape(nblocks, 3)
    block = jnp.arange(nblocks)
    left = jnp.where(block == 0, jnp.where(my_z == 0, YP * 8 + 5, L1 * 8 + nblocks - 1), block - 1)
    right = jnp.where(block == nblocks - 1, jnp.where(my_z == NZ - 1, YM * 8 + 5, R1 * 8), block + 1)
    codes = jnp.concatenate([jnp.stack([left, block, right], axis=1), rand_code], axis=1).reshape(-1)
    edges = jnp.stack([me == 0, me == nctx - 1]).astype(jnp.int32)
    piece_rows = ((my_y - arange4) & (NY - 1)) * (BS // NY)
    return picks, jnp.concatenate([codes, edges, piece_rows]).astype(jnp.int32)


def whole_step(queries, key_value, lanczos_vec, rand_blocks, global_ids):
    rows, width = queries.shape
    nblocks = rows // BS
    nctx = lax.axis_size("ctx")
    nhead = lax.axis_size("head")
    me = lax.axis_index("ctx")
    picks, codes = tables(rand_blocks, global_ids, me, nblocks, nctx)
    blocks = key_value.reshape(2, nblocks, BS, width)
    piece = (2, 2, BS // NY, width)
    quarters = pack(split_kernel, picks, (blocks,), (piece,) * NY, 8)
    held = (quarters[0], send(quarters[1], y_shift(1)), send(quarters[2], y_shift(2)), send(quarters[3], y_shift(-1)))
    (mine,) = pack(functools.partial(choose_kernel, 33), picks, held, (piece,), 2)
    ring = [mine]
    for _ in range(1, 5):
        ring.append(send(ring[-1], z_shift(1)))
    back = [mine]
    for _ in range(1, 4):
        back.append(send(back[-1], z_shift(-1)))
    (quarter,) = pack(functools.partial(choose_kernel, 35), picks, tuple(ring) + tuple(back[:0:-1]), (piece,), 2)
    pieces = (quarter, send(quarter, y_shift(1)), send(quarter, y_shift(2)), send(quarter, y_shift(-1)))
    products = []
    stats = []
    for k, (first, heads) in enumerate(CHUNKS):
        cw = heads * HD
        own = jnp.swapaxes(blocks[..., first * HD : first * HD + cw], 0, 1)

        def slots(count, cw=cw):
            return (count, 2, BS, cw)

        l1 = send(own, z_shift(1))
        r1 = send(own, z_shift(-1))
        l2 = send(l1, z_shift(1))
        r2 = send(r1, z_shift(-1))
        plus, minus, ep, e2, em = pack(
            near_kernel, picks, (own, l1, r1, l2, r2),
            (slots(6), slots(6), slots(6), slots(5), slots(6)), 29,
        )
        a3 = send(plus, z_shift(1))
        b3 = send(minus, z_shift(-1))
        a4 = send(a3[4:6], z_shift(1))
        b4 = send(b3[4:6], z_shift(-1))
        yp = send(ep, y_shift(1))
        y2 = send(e2, y_shift(2))
        ym = send(em, y_shift(-1))
        fp, f2, fm = pack(late_kernel, picks, (a3, b3, a4, b4), (slots(3),) * 3, 9)
        lyp = send(fp, y_shift(1))
        ly2 = send(f2, y_shift(2))
        lym = send(fm, y_shift(-1))
        arrays = (own, l1, l2, a3, a4, b3, r2, r1, yp, ym, y2, lyp, lym, ly2) + pieces
        keys = LIST * BS
        parts = SPLIT[k]
        for part in range(parts):
            steps = nblocks // parts
            base = part * steps
            col_spec = pl.BlockSpec((BS, cw), lambda b, *_, at=first // heads, base=base: (b + base, at))
            product, stat = pl.pallas_call(
                functools.partial(attention_kernel, nblocks, (first, len(stats)), base),
                out_shape=(
                    jax.ShapeDtypeStruct((steps * BS, cw), jnp.float32),
                    jax.ShapeDtypeStruct((8, 128), jnp.float32),
                ),
                grid_spec=pltpu.PrefetchScalarGridSpec(
                    num_scalar_prefetch=1,
                    grid=(steps,),
                    in_specs=[col_spec, col_spec] + [ANY] * len(arrays),
                    out_specs=(
                        pl.BlockSpec((BS, cw), lambda b, *_: (b, 0)),
                        pl.BlockSpec((8, 128), lambda b, *_: (0, 0)),
                    ),
                    scratch_shapes=[
                        pltpu.VMEM((2, 2, keys, cw), jnp.bfloat16),
                        pltpu.SemaphoreType.DMA((2, 2 * LIST)),
                        pltpu.VMEM((steps, 8, cw), jnp.float32),
                    ],
                ),
                cost_estimate=pl.CostEstimate(
                    flops=10 * steps * BS * keys * cw, bytes_accessed=16 * steps * BS * cw,
                    transcendentals=steps * BS * keys * heads,
                ),
            )(codes, queries, lanczos_vec, *arrays)
            products.append(product)
            stats.append(stat)
    sent = jnp.broadcast_to(sum(stats)[:1], (nctx * nhead, 128))
    gathered = lax.all_to_all(sent, ("ctx", "head"), 0, 0, tiled=True)
    count = float(rows * width * nctx * nhead)
    step = rows // 4
    fin_spec = pl.BlockSpec((step, width), lambda i: (i, 0))
    part_specs = []
    for (_, heads), parts in zip(CHUNKS, SPLIT):
        per = 4 // parts
        for part in range(parts):
            part_specs.append(
                pl.BlockSpec(
                    (step, heads * HD),
                    lambda i, part=part, per=per: (jnp.clip(i - part * per, 0, per - 1), 0),
                )
            )
    next_vec, coef = pl.pallas_call(
        functools.partial(finish_kernel, count),
        out_shape=(
            jax.ShapeDtypeStruct((rows, width), jnp.float32),
            jax.ShapeDtypeStruct((8, 128), jnp.float32),
        ),
        grid=(4,),
        in_specs=[pl.BlockSpec((nctx * nhead, 128), lambda i: (0, 0))] + part_specs + [fin_spec],
        out_specs=(fin_spec, pl.BlockSpec((8, 128), lambda i: (0, 0))),
        scratch_shapes=[pltpu.VMEM((8, 128), jnp.float32)],
        name="finish",
    )(gathered, *products, lanczos_vec)
    return next_vec, coef[0, :2]


def solution(mesh):
    placed = (P("ctx", "head"), P(None, "ctx", "head"), P("ctx", "head"), P(), P())
    return jax.shard_map(whole_step, mesh=mesh, in_specs=placed, out_specs=(P("ctx", "head"), P()), check_vma=False)
```

```python
import functools

import jax
import jax.numpy as jnp
from jax import lax
from jax.experimental import pallas as pl
from jax.experimental.pallas import tpu as pltpu
from jax.sharding import PartitionSpec as P


HD = 128
BS = 128
LIST = 8
SCALE = HD ** (-0.5)
LOG2E = 1.4426950408889634
NT = (((1,), (1,)), ((), ()))


def attend_tile(q, tangent, keys, values, left_bias, right_bias):
    both = jnp.concatenate([q, tangent], axis=0)
    logits = lax.dot_general(both, keys, NT, preferred_element_type=jnp.float32)
    scores = logits[:BS]
    dots = logits[BS:]
    scores = jnp.concatenate(
        [
            scores[:, :BS] + left_bias,
            scores[:, BS : 2 * BS],
            scores[:, 2 * BS : 3 * BS] + right_bias,
            scores[:, 3 * BS :],
        ],
        axis=1,
    )
    row_top = jnp.max(scores, axis=1, keepdims=True)
    weights = jnp.exp2((scores - row_top) * (SCALE * LOG2E))
    inv_total = 1.0 / jnp.sum(weights, axis=1, keepdims=True)
    prob = weights * inv_total
    center = jnp.sum(prob * dots, axis=1, keepdims=True)
    first = ((prob * SCALE) * (dots - center)).astype(jnp.bfloat16)
    dout = jnp.dot(first, values, preferred_element_type=jnp.float32).astype(jnp.bfloat16)
    dprob = lax.dot_general(dout, values, NT, preferred_element_type=jnp.float32)
    center_two = jnp.sum(prob * dprob, axis=1, keepdims=True)
    second = (prob * (dprob - center_two)).astype(jnp.bfloat16)
    return jnp.dot(second, keys, preferred_element_type=jnp.float32) * SCALE


NY, NZ = 4, 8
CHUNKS = ((0, 2), (2, 2))
CALLS = len(CHUNKS)
OWN, L1, _, _, _, _, _, R1, YP, YM, _, LYP, _, _, MP, _, _ = range(17)


def start_choice(arrays, ids, code, dst, sem):
    which = lax.shift_right_logical(code, 3)
    slot = code & 7
    for k in ids:
        @pl.when(which == k)
        def _(k=k):
            pltpu.make_async_copy(arrays[k].at[slot], dst, sem).start()


def attention_kernel(nblocks, chunk, narrays, code_ref, q_ref, vec_ref, *refs):
    arrays = refs[:narrays]
    pieces = refs[narrays : narrays + NY]
    out_ref, stat_ref, kvbuf, sems, acc = refs[narrays + NY :]
    b = pl.program_id(0)
    width = q_ref.shape[1]
    table = nblocks * 6
    listed = (0, 1, 2, 5, 6, 7)

    def place(slot, pos):
        return kvbuf.at[slot, :, pl.ds(pos * BS, BS)]

    def globals_in(slot):
        copies = []
        cols = pl.ds(chunk[0] * HD, width)
        for i in range(NY):
            rows = pl.multiple_of(code_ref[table + 2 + i], BS // NY)
            for g in range(2):
                dst = kvbuf.at[slot, :, pl.ds((3 + g) * BS + rows, BS // NY)]
                sem = sems.at[slot, LIST + 2 * i + g]
                copies.append(pltpu.make_async_copy(pieces[i].at[g, :, :, cols], dst, sem))
        return copies

    def start(blk, slot):
        for j, pos in enumerate(listed):
            ids = (
                (OWN, L1, YP) if pos == 0 else (OWN,) if pos == 1 else (OWN, R1, YM) if pos == 2
                else tuple(range(narrays))
            )
            start_choice(arrays, ids, code_ref[blk * 6 + j], place(slot, pos), sems.at[slot, pos])

        @pl.when(blk < 2)
        def _():
            for cp in globals_in(slot):
                cp.start()

    slot = lax.rem(b, 2)

    @pl.when(b == 0)
    def _():
        start(0, 0)

    @pl.when(b + 1 < nblocks)
    def _():
        start(b + 1, 1 - slot)

    for pos in listed:
        pltpu.make_async_copy(arrays[OWN].at[0], place(slot, pos), sems.at[slot, pos]).wait()

    @pl.when(b < 2)
    def _():
        for cp in globals_in(slot):
            cp.wait()

    left_bias = jnp.where((b == 0) & (code_ref[table] == 1), -1e30, 0.0).astype(jnp.float32)
    right_bias = jnp.where((b == nblocks - 1) & (code_ref[table + 1] == 1), -1e30, 0.0).astype(jnp.float32)
    for h in range(width // HD):
        cols = slice(h * HD, (h + 1) * HD)
        vec = vec_ref[:, cols]
        prod = attend_tile(
            q_ref[:, cols], vec.astype(jnp.bfloat16), kvbuf[slot, 0, :, cols], kvbuf[slot, 1, :, cols],
            left_bias, right_bias,
        )
        out_ref[:, cols] = prod
        s = jnp.sum(vec * vec, axis=0, keepdims=True)
        c = jnp.sum(vec * prod, axis=0, keepdims=True)
        a = jnp.where(s > 0, c / jnp.where(s > 0, s, 1.0), 0.0)
        d = prod - a * vec
        acc[b, 0:1, cols] = s
        acc[b, 1:2, cols] = c
        acc[b, 2:3, cols] = jnp.sum(d * d, axis=0, keepdims=True)

    @pl.when(b == nblocks - 1)
    def _():
        s, c, r = combine(acc[:, 0, :], acc[:, 1, :], acc[:, 2, :])
        lane = lax.broadcasted_iota(jnp.int32, stat_ref.shape, 1) - 3 * chunk[1]
        stat_ref[...] = jnp.where(lane == 0, s, jnp.where(lane == 1, c, jnp.where(lane == 2, r, 0.0)))


def run_copies(plan, sems):
    copies = [pltpu.make_async_copy(src, dst, sems.at[i]) for i, (src, dst) in enumerate(plan)]
    for cp in copies:
        cp.start()
    for cp in copies:
        cp.wait()


def near_kernel(pick_ref, own, l1, r1, l2, r2, plus, minus, yp, y2, ym, sems):
    plan = []
    for i in range(6):
        plan.append((l2.at[pick_ref[i]], plus.at[i]))
        plan.append((r2.at[pick_ref[6 + i]], minus.at[i]))
    for row, out in enumerate((yp, y2, ym)):
        for i, src in enumerate((own, l1, r1, l2, r2)):
            plan.append((src.at[pick_ref[12 + row * 5 + i]], out.at[i]))
    plan.append((l1.at[l1.shape[0] - 1], yp.at[5]))
    plan.append((r1.at[0], ym.at[5]))
    run_copies(plan, sems)


def first_kernel(pick_ref, own, l1, r1, yp, y2, ym, sems):
    plan = []
    for row, out in enumerate((yp, y2, ym)):
        for i, src in enumerate((own, l1, r1)):
            plan.append((src.at[pick_ref[12 + row * 5 + i]], out.at[i]))
    plan.append((l1.at[l1.shape[0] - 1], yp.at[3]))
    plan.append((r1.at[0], ym.at[3]))
    run_copies(plan, sems)


def third_kernel(pick_ref, l2, r2, plus, minus, sems):
    plan = []
    for i in range(6):
        plan.append((l2.at[pick_ref[i]], plus.at[i]))
        plan.append((r2.at[pick_ref[6 + i]], minus.at[i]))
    run_copies(plan, sems)


def late_kernel(pick_ref, a3, b3, a4, b4, *refs):
    second = refs[:-4]
    outs, sems = refs[-4:-1], refs[-1]
    last = (a4.at[1], b4.at[0], b4.at[1])
    plan = []
    for row, out in enumerate(outs):
        plan += [(a3.at[row + 1], out.at[0]), (b3.at[row + 1], out.at[1]), (last[row], out.at[2])]
        for i, src in enumerate(second):
            plan.append((src.at[pick_ref[12 + row * 5 + 3 + i]], out.at[3 + i]))
    run_copies(plan, sems)


def split_kernel(pick_ref, blocks, p0, p1, p2, p3, sems):
    plan = []
    for i, out in enumerate((p0, p1, p2, p3)):
        rows = pl.ds(pl.multiple_of(pick_ref[29 + i], BS // NY), BS // NY)
        for g in range(2):
            plan.append((blocks.at[:, pick_ref[27 + g], rows], out.at[g]))
    run_copies(plan, sems)


def choose_kernel(at, pick_ref, *refs):
    srcs, out, sems = refs[:-2], refs[-2], refs[-1]
    for g in range(2):
        for k, src in enumerate(srcs):
            @pl.when(pick_ref[at + g] == k)
            def _(src=src, g=g):
                pltpu.make_async_copy(src.at[g], out.at[g], sems.at[g]).start()
    for g in range(2):
        pltpu.make_async_copy(srcs[0].at[g], out.at[g], sems.at[g]).wait()


def total(x):
    return jnp.sum(jnp.sum(x, axis=0, keepdims=True), axis=1, keepdims=True)


def combine(s, c, r):
    s_all = total(s)
    c_all = total(c)
    a = jnp.where(s > 0, c / jnp.where(s > 0, s, 1.0), 0.0)
    a_all = jnp.where(s_all > 0, c_all / jnp.where(s_all > 0, s_all, 1.0), 0.0)
    gap = a - a_all
    return s_all, c_all, total(r + (s * gap) * gap)


def finish_kernel(count, gathered, *refs):
    prods = refs[:CALLS]
    vec_ref, out_ref, coef_ref, ab = refs[CALLS:]
    step = pl.program_id(0)

    @pl.when(step == 0)
    def _():
        table = gathered[...]
        parts = [[table[:, 3 * k + i : 3 * k + i + 1] for i in range(3)] for k in range(CALLS)]
        alpha = sum(total(c) for _, c, _ in parts) * (1.0 / count)
        square = 0.0
        for s, c, r in parts:
            gap = jnp.where(s > 0, c / jnp.where(s > 0, s, 1.0), 0.0) - alpha
            square = square + total(r + (s * gap) * gap)
        beta = jnp.sqrt(square * (1.0 / count) + 1e-06)
        ab[0:1, :] = jnp.broadcast_to(alpha, (1, 128))
        ab[1:2, :] = jnp.broadcast_to(1.0 / beta, (1, 128))
        lane = lax.broadcasted_iota(jnp.int32, coef_ref.shape, 1)
        coef_ref[...] = jnp.where(lane == 0, alpha, beta)

    alpha = ab[0:1, 0:1]
    inv = ab[1:2, 0:1]
    for (first, heads), prod in zip(CHUNKS, prods):
        cols = slice(first * HD, (first + heads) * HD)
        out_ref[:, cols] = (prod[...] - alpha * vec_ref[:, cols]) * inv


def z_shift(d):
    return [(y * NZ + z, y * NZ + (z + d) % NZ) for y in range(NY) for z in range(NZ)]


def y_shift(d):
    return [(y * NZ + z, (y + d) % NY * NZ + z) for y in range(NY) for z in range(NZ)]


def send(x, pairs):
    return lax.ppermute(x, "ctx", pairs)


ANY = pl.BlockSpec(memory_space=pltpu.HBM)


def pack(kernel, picks, arrays, shapes, ncopies):
    return pl.pallas_call(
        kernel,
        out_shape=tuple(jax.ShapeDtypeStruct(shape, jnp.bfloat16) for shape in shapes),
        grid_spec=pltpu.PrefetchScalarGridSpec(
            num_scalar_prefetch=1,
            grid=(),
            in_specs=[ANY] * len(arrays),
            out_specs=tuple(pl.BlockSpec(memory_space=pltpu.VMEM) for _ in shapes),
            scratch_shapes=[pltpu.SemaphoreType.DMA((ncopies,))],
        ),
        cost_estimate=pl.CostEstimate(flops=0, bytes_accessed=6000000, transcendentals=0),
    )(picks, *arrays)


def tables(rand_blocks, global_ids, me, nblocks, nctx):
    my_y, my_z = me // NZ, me % NZ
    requests = rand_blocks.reshape(nctx, nblocks * 3)
    mine = lax.dynamic_index_in_dim(requests, me, 0, keepdims=False)
    pairs = [(i, 1, -2) for i in range(4)] + [(0, 2, -2), (1, 2, -2)]
    pairs += [(i, -1, 2) for i in range(4)] + [(2, -2, 2), (3, -2, 2)]
    for row in (1, 2, 3):
        pairs += [(row, 0, d) for d in (0, -1, 1, -2, 2)]
    offsets = jnp.array(pairs, jnp.int32)
    consumer = ((my_y + offsets[:, 0]) & (NY - 1)) * NZ + ((my_z + offsets[:, 1]) & (NZ - 1))
    source = my_y * NZ + ((my_z + offsets[:, 2]) & (NZ - 1))
    shift = nblocks.bit_length() - 1
    wanted = requests[consumer]
    picks = jnp.sum(
        jnp.where((wanted >> shift) == source[:, None], wanted & (nblocks - 1), 0), axis=1
    )
    g_shard = global_ids >> shift
    g_y, g_z = g_shard >> 3, g_shard & (NZ - 1)
    arange4 = jnp.arange(NY)
    picks = jnp.concatenate(
        [
            picks,
            global_ids & (nblocks - 1),
            ((my_y + arange4) & (NY - 1)) * (BS // NY),
            (my_y - g_y) & (NY - 1),
            (my_z - g_z) & (NZ - 1),
        ]
    ).astype(jnp.int32)
    src = mine >> shift
    inside = mine & (nblocks - 1)
    dy = ((src >> 3) - my_y) & (NY - 1)
    dz = (my_z - src) & (NZ - 1)
    late = (dz >= 3) & (dz <= 5)
    near_slot = jnp.where(late, 0, inside)
    order = jnp.where(
        late, jnp.where(dz == 3, 0, jnp.where(dz == 5, 1, 2)),
        jnp.where(dz == 0, 0, jnp.where(dz == 1, 1, jnp.where(dz == 7, 2, jnp.where(dz == 2, 3, 4)))),
    )
    row = jnp.where(dy == 1, 1, jnp.where(dy == 2, 2, 0))
    second = (dz == 2) | (dz == 6)
    block = jnp.arange(nblocks)
    edges = jnp.stack([me == 0, me == nctx - 1]).astype(jnp.int32)
    piece_rows = ((my_y - arange4) & (NY - 1)) * (BS // NY)
    codes = []
    for chunk, edge_slot in ((0, 5), (1, 3)):
        far = YP + row + jnp.where(late, LYP - YP, 0)
        if chunk:
            far = jnp.where(second, MP + row, far)
        rand_code = jnp.where(dy == 0, dz * 8 + near_slot, far * 8 + order).reshape(nblocks, 3)
        left = jnp.where(
            block == 0, jnp.where(my_z == 0, YP * 8 + edge_slot, L1 * 8 + nblocks - 1), block - 1
        )
        right = jnp.where(
            block == nblocks - 1, jnp.where(my_z == NZ - 1, YM * 8 + edge_slot, R1 * 8), block + 1
        )
        listed = jnp.concatenate([jnp.stack([left, block, right], axis=1), rand_code], axis=1)
        codes.append(jnp.concatenate([listed.reshape(-1), edges, piece_rows]).astype(jnp.int32))
    return picks, codes


def whole_step(queries, key_value, lanczos_vec, rand_blocks, global_ids):
    rows, width = queries.shape
    nblocks = rows // BS
    nctx = lax.axis_size("ctx")
    nhead = lax.axis_size("head")
    me = lax.axis_index("ctx")
    picks, codes = tables(rand_blocks, global_ids, me, nblocks, nctx)
    blocks = key_value.reshape(2, nblocks, BS, width)
    piece = (2, 2, BS // NY, width)
    quarters = pack(split_kernel, picks, (blocks,), (piece,) * NY, 8)
    held = (
        quarters[0],
        send(quarters[1], y_shift(1)),
        send(quarters[2], y_shift(2)),
        send(quarters[3], y_shift(-1)),
    )
    (mine,) = pack(functools.partial(choose_kernel, 33), picks, held, (piece,), 2)
    from_left = send(mine, z_shift(1))
    from_right = send(mine, z_shift(-1))
    (close,) = pack(
        functools.partial(choose_kernel, 35), picks,
        (mine, from_left, mine, mine, mine, mine, mine, from_right), (piece,), 2,
    )
    hop_left = send(close, z_shift(3))
    hop_right = send(close, z_shift(-3))
    (quarter,) = pack(
        functools.partial(choose_kernel, 35), picks,
        (close, close, hop_left, hop_left, hop_left, hop_right, hop_right, close), (piece,), 2,
    )
    pieces = (
        quarter, send(quarter, y_shift(1)), send(quarter, y_shift(2)), send(quarter, y_shift(-1))
    )
    cw = CHUNKS[0][1] * HD

    def slots(count):
        return (count, 2, BS, cw)

    def rows_of(packed):
        return tuple(send(x, y_shift(d)) for x, d in zip(packed, (1, 2, -1)))

    own, l1, r1, l2, r2 = [], [], [], [], []
    for k, (first, heads) in enumerate(CHUNKS):
        own.append(jnp.swapaxes(blocks[..., first * HD : (first + heads) * HD], 0, 1))
        l1.append(send(own[k], z_shift(1)))
        r1.append(send(own[k], z_shift(-1)))
        l2.append(send(l1[k], z_shift(1)))
        r2.append(send(r1[k], z_shift(-1)))
    plus, minus, *early = pack(
        near_kernel, picks, (own[0], l1[0], r1[0], l2[0], r2[0]),
        (slots(6), slots(6), slots(6), slots(5), slots(6)), 29,
    )
    y0 = rows_of(early)
    a3, b3 = send(plus, z_shift(1)), send(minus, z_shift(-1))
    a4, b4 = send(a3[4:6], z_shift(1)), send(b3[4:6], z_shift(-1))
    early = pack(first_kernel, picks, (own[1], l1[1], r1[1]), (slots(4), slots(3), slots(4)), 11)
    y1 = rows_of(early)
    plus, minus = pack(third_kernel, picks, (l2[1], r2[1]), (slots(6), slots(6)), 12)
    mid = rows_of(pack(late_kernel, picks, (a3, b3, a4, b4, l2[1], r2[1]), (slots(5),) * 3, 15))
    c3, d3 = send(plus, z_shift(1)), send(minus, z_shift(-1))
    c4, d4 = send(c3[4:6], z_shift(1)), send(d3[4:6], z_shift(-1))
    last = rows_of(pack(late_kernel, picks, (c3, d3, c4, d4), (slots(3),) * 3, 9))

    def by_code(y):
        return (y[0], y[2], y[1])

    sources = (
        (own[0], l1[0], l2[0], a3, a4, b3, r2[0], r1[0]) + by_code(y0) + by_code(mid),
        (own[1], l1[1], l2[1], c3, c4, d3, r2[1], r1[1]) + by_code(y1) + by_code(last) + by_code(mid),
    )
    products = []
    stats = []
    keys = LIST * BS
    for k, arrays in enumerate(sources):
        product, stat = pl.pallas_call(
            functools.partial(attention_kernel, nblocks, (CHUNKS[k][0], k), len(arrays)),
            out_shape=(
                jax.ShapeDtypeStruct((rows, cw), jnp.float32),
                jax.ShapeDtypeStruct((8, 128), jnp.float32),
            ),
            grid_spec=pltpu.PrefetchScalarGridSpec(
                num_scalar_prefetch=1,
                grid=(nblocks,),
                in_specs=[pl.BlockSpec((BS, cw), lambda b, *_, k=k: (b, k))] * 2
                + [ANY] * (len(arrays) + NY),
                out_specs=(
                    pl.BlockSpec((BS, cw), lambda b, *_: (b, 0)),
                    pl.BlockSpec((8, 128), lambda b, *_: (0, 0)),
                ),
                scratch_shapes=[
                    pltpu.VMEM((2, 2, keys, cw), jnp.bfloat16),
                    pltpu.SemaphoreType.DMA((2, 2 * LIST)),
                    pltpu.VMEM((nblocks, 8, cw), jnp.float32),
                ],
            ),
            cost_estimate=pl.CostEstimate(
                flops=10 * rows * keys * cw, bytes_accessed=16 * rows * cw,
                transcendentals=rows * keys * (cw // HD),
            ),
        )(codes[k], queries, lanczos_vec, *arrays, *pieces)
        products.append(product)
        stats.append(stat)
    sent = jnp.broadcast_to(sum(stats)[:1], (nctx * nhead, 128))
    gathered = lax.all_to_all(sent, ("ctx", "head"), 0, 0, tiled=True)
    count = float(rows * width * nctx * nhead)
    step = rows // 4
    fin_spec = pl.BlockSpec((step, width), lambda i: (i, 0))
    part_specs = [pl.BlockSpec((step, heads * HD), lambda i: (i, 0)) for _, heads in CHUNKS]
    next_vec, coef = pl.pallas_call(
        functools.partial(finish_kernel, count),
        out_shape=(
            jax.ShapeDtypeStruct((rows, width), jnp.float32),
            jax.ShapeDtypeStruct((8, 128), jnp.float32),
        ),
        grid=(4,),
        in_specs=[pl.BlockSpec((nctx * nhead, 128), lambda i: (0, 0))] + part_specs + [fin_spec],
        out_specs=(fin_spec, pl.BlockSpec((8, 128), lambda i: (0, 0))),
        scratch_shapes=[pltpu.VMEM((8, 128), jnp.float32)],
        name="finish",
    )(gathered, *products, lanczos_vec)
    return next_vec, coef[0, :2]


def solution(mesh):
    placed = (P("ctx", "head"), P(None, "ctx", "head"), P("ctx", "head"), P(), P())
    return jax.shard_map(
        whole_step, mesh=mesh, in_specs=placed, out_specs=(P("ctx", "head"), P()), check_vma=False
    )
```

```python
import functools

import jax
import jax.numpy as jnp
from jax import lax
from jax.experimental import pallas as pl
from jax.experimental.pallas import tpu as pltpu
from jax.sharding import PartitionSpec as P


HD = 128
BS = 128
LIST = 8
SCALE = HD ** (-0.5)
LOG2E = 1.4426950408889634
NT = (((1,), (1,)), ((), ()))


def attend_tiles(tiles, left_bias, right_bias):
    count = range(len(tiles))
    logits = [
        lax.dot_general(
            jnp.concatenate([q, tangent], axis=0), keys, NT, preferred_element_type=jnp.float32
        )
        for q, tangent, keys, _ in tiles
    ]
    prob, dots = [], []
    for x in logits:
        scores = x[:BS]
        scores = jnp.concatenate(
            [
                scores[:, :BS] + left_bias,
                scores[:, BS : 2 * BS],
                scores[:, 2 * BS : 3 * BS] + right_bias,
                scores[:, 3 * BS :],
            ],
            axis=1,
        )
        row_top = jnp.max(scores, axis=1, keepdims=True)
        weights = jnp.exp2((scores - row_top) * (SCALE * LOG2E))
        prob.append(weights * (1.0 / jnp.sum(weights, axis=1, keepdims=True)))
        dots.append(x[BS:])
    dout = []
    for i in count:
        center = jnp.sum(prob[i] * dots[i], axis=1, keepdims=True)
        first = ((prob[i] * SCALE) * (dots[i] - center)).astype(jnp.bfloat16)
        dout.append(jnp.dot(first, tiles[i][3], preferred_element_type=jnp.float32).astype(jnp.bfloat16))
    dprob = [
        lax.dot_general(dout[i], tiles[i][3], NT, preferred_element_type=jnp.float32) for i in count
    ]
    out = []
    for i in count:
        center = jnp.sum(prob[i] * dprob[i], axis=1, keepdims=True)
        second = (prob[i] * (dprob[i] - center)).astype(jnp.bfloat16)
        out.append(jnp.dot(second, tiles[i][2], preferred_element_type=jnp.float32) * SCALE)
    return out


NY, NZ = 4, 8
CHUNKS = ((0, 2), (2, 2))
CALLS = len(CHUNKS)
OWN, L1, _, _, _, _, _, R1, YP, YM, _, LYP, _, _, MP, _, _ = range(17)


def start_choice(arrays, ids, code, dst, sem):
    which = lax.shift_right_logical(code, 3)
    slot = code & 7
    for k in ids:
        @pl.when(which == k)
        def _(k=k):
            pltpu.make_async_copy(arrays[k].at[slot], dst, sem).start()


def attention_kernel(nblocks, chunk, narrays, code_ref, q_ref, vec_ref, *refs):
    arrays = refs[:narrays]
    pieces = refs[narrays : narrays + NY]
    out_ref, stat_ref, kvbuf, sems, acc = refs[narrays + NY :]
    b = pl.program_id(0)
    width = q_ref.shape[1]
    table = nblocks * 6
    listed = (0, 1, 2, 5, 6, 7)

    def place(slot, pos):
        return kvbuf.at[slot, :, pl.ds(pos * BS, BS)]

    def globals_in(slot):
        copies = []
        cols = pl.ds(chunk[0] * HD, width)
        for i in range(NY):
            rows = pl.multiple_of(code_ref[table + 2 + i], BS // NY)
            for g in range(2):
                dst = kvbuf.at[slot, :, pl.ds((3 + g) * BS + rows, BS // NY)]
                sem = sems.at[slot, LIST + 2 * i + g]
                copies.append(pltpu.make_async_copy(pieces[i].at[g, :, :, cols], dst, sem))
        return copies

    def start(blk, slot):
        for j, pos in enumerate(listed):
            ids = (
                (OWN, L1, YP) if pos == 0 else (OWN,) if pos == 1 else (OWN, R1, YM) if pos == 2
                else tuple(range(narrays))
            )
            start_choice(arrays, ids, code_ref[blk * 6 + j], place(slot, pos), sems.at[slot, pos])

        @pl.when(blk < 2)
        def _():
            for cp in globals_in(slot):
                cp.start()

    slot = lax.rem(b, 2)

    @pl.when(b == 0)
    def _():
        start(0, 0)

    @pl.when(b + 1 < nblocks)
    def _():
        start(b + 1, 1 - slot)

    for pos in listed:
        pltpu.make_async_copy(arrays[OWN].at[0], place(slot, pos), sems.at[slot, pos]).wait()

    @pl.when(b < 2)
    def _():
        for cp in globals_in(slot):
            cp.wait()

    left_bias = jnp.where((b == 0) & (code_ref[table] == 1), -1e30, 0.0).astype(jnp.float32)
    right_bias = jnp.where((b == nblocks - 1) & (code_ref[table + 1] == 1), -1e30, 0.0).astype(jnp.float32)
    heads = [slice(h * HD, (h + 1) * HD) for h in range(width // HD)]
    tiles = [
        (
            q_ref[:, cols], vec_ref[:, cols].astype(jnp.bfloat16),
            kvbuf[slot, 0, :, cols], kvbuf[slot, 1, :, cols],
        )
        for cols in heads
    ]
    for cols, prod in zip(heads, attend_tiles(tiles, left_bias, right_bias)):
        vec = vec_ref[:, cols]
        out_ref[:, cols] = prod
        s = jnp.sum(vec * vec, axis=0, keepdims=True)
        c = jnp.sum(vec * prod, axis=0, keepdims=True)
        a = jnp.where(s > 0, c / jnp.where(s > 0, s, 1.0), 0.0)
        d = prod - a * vec
        acc[b, 0:1, cols] = s
        acc[b, 1:2, cols] = c
        acc[b, 2:3, cols] = jnp.sum(d * d, axis=0, keepdims=True)

    @pl.when(b == nblocks - 1)
    def _():
        s, c, r = combine(acc[:, 0, :], acc[:, 1, :], acc[:, 2, :])
        lane = lax.broadcasted_iota(jnp.int32, stat_ref.shape, 1) - 3 * chunk[1]
        stat_ref[...] = jnp.where(lane == 0, s, jnp.where(lane == 1, c, jnp.where(lane == 2, r, 0.0)))


def run_copies(plan, sems):
    copies = [pltpu.make_async_copy(src, dst, sems.at[i]) for i, (src, dst) in enumerate(plan)]
    for cp in copies:
        cp.start()
    for cp in copies:
        cp.wait()


def first_kernel(pick_ref, own_a, l1_a, r1_a, own_b, l1_b, r1_b, yp, y2, ym, sems):
    plan = []
    for k, arrays in enumerate(((own_a, l1_a, r1_a), (own_b, l1_b, r1_b))):
        for row, (out, step) in enumerate(((yp, 4), (y2, 3), (ym, 4))):
            for i, src in enumerate(arrays):
                plan.append((src.at[pick_ref[12 + row * 5 + i]], out.at[k * step + i]))
        plan.append((arrays[1].at[own_a.shape[0] - 1], yp.at[k * 4 + 3]))
        plan.append((arrays[2].at[0], ym.at[k * 4 + 3]))
    run_copies(plan, sems)


def third_hop(pick_ref, l2, r2, plus, minus):
    plan = []
    for i in range(6):
        plan.append((l2.at[pick_ref[i]], plus.at[i]))
        plan.append((r2.at[pick_ref[6 + i]], minus.at[i]))
    return plan


def third_kernel(pick_ref, l2, r2, plus, minus, sems):
    run_copies(third_hop(pick_ref, l2, r2, plus, minus), sems)


def second_kernel(pick_ref, l2_a, r2_a, l2_b, r2_b, plus, minus, yp, y2, ym, sems):
    plan = third_hop(pick_ref, l2_b, r2_b, plus, minus)
    for row, out in enumerate((yp, y2, ym)):
        for i, src in enumerate((l2_a, r2_a, l2_b, r2_b)):
            plan.append((src.at[pick_ref[12 + row * 5 + 3 + i % 2]], out.at[i]))
    run_copies(plan, sems)


def late_kernel(a3, b3, a4, b4, yp, y2, ym, sems):
    last = (a4.at[1], b4.at[0], b4.at[1])
    plan = []
    for row, out in enumerate((yp, y2, ym)):
        plan += [(a3.at[row + 1], out.at[0]), (b3.at[row + 1], out.at[1]), (last[row], out.at[2])]
    run_copies(plan, sems)


def split_kernel(pick_ref, blocks, p0, p1, p2, p3, sems):
    plan = []
    for i, out in enumerate((p0, p1, p2, p3)):
        rows = pl.ds(pl.multiple_of(pick_ref[29 + i], BS // NY), BS // NY)
        for g in range(2):
            plan.append((blocks.at[:, pick_ref[27 + g], rows], out.at[g]))
    run_copies(plan, sems)


def choose_kernel(at, pick_ref, *refs):
    srcs, out, sems = refs[:-2], refs[-2], refs[-1]
    for g in range(2):
        for k, src in enumerate(srcs):
            @pl.when(pick_ref[at + g] == k)
            def _(src=src, g=g):
                pltpu.make_async_copy(src.at[g], out.at[g], sems.at[g]).start()
    for g in range(2):
        pltpu.make_async_copy(srcs[0].at[g], out.at[g], sems.at[g]).wait()


def total(x):
    return jnp.sum(jnp.sum(x, axis=0, keepdims=True), axis=1, keepdims=True)


def combine(s, c, r):
    s_all = total(s)
    c_all = total(c)
    a = jnp.where(s > 0, c / jnp.where(s > 0, s, 1.0), 0.0)
    a_all = jnp.where(s_all > 0, c_all / jnp.where(s_all > 0, s_all, 1.0), 0.0)
    gap = a - a_all
    return s_all, c_all, total(r + (s * gap) * gap)


def finish_kernel(count, gathered, *refs):
    prods = refs[:CALLS]
    vec_ref, out_ref, coef_ref, ab = refs[CALLS:]
    step = pl.program_id(0)

    @pl.when(step == 0)
    def _():
        table = gathered[...]
        parts = [[table[:, 3 * k + i : 3 * k + i + 1] for i in range(3)] for k in range(CALLS)]
        alpha = sum(total(c) for _, c, _ in parts) * (1.0 / count)
        square = 0.0
        for s, c, r in parts:
            gap = jnp.where(s > 0, c / jnp.where(s > 0, s, 1.0), 0.0) - alpha
            square = square + total(r + (s * gap) * gap)
        beta = jnp.sqrt(square * (1.0 / count) + 1e-06)
        ab[0:1, :] = jnp.broadcast_to(alpha, (1, 128))
        ab[1:2, :] = jnp.broadcast_to(1.0 / beta, (1, 128))
        lane = lax.broadcasted_iota(jnp.int32, coef_ref.shape, 1)
        coef_ref[...] = jnp.where(lane == 0, alpha, beta)

    alpha = ab[0:1, 0:1]
    inv = ab[1:2, 0:1]
    for (first, heads), prod in zip(CHUNKS, prods):
        cols = slice(first * HD, (first + heads) * HD)
        out_ref[:, cols] = (prod[...] - alpha * vec_ref[:, cols]) * inv


def z_shift(d):
    return [(y * NZ + z, y * NZ + (z + d) % NZ) for y in range(NY) for z in range(NZ)]


def y_shift(d):
    return [(y * NZ + z, (y + d) % NY * NZ + z) for y in range(NY) for z in range(NZ)]


def send(x, pairs):
    return lax.ppermute(x, "ctx", pairs)


ANY = pl.BlockSpec(memory_space=pltpu.HBM)


def pack(kernel, picks, arrays, shapes, ncopies):
    scalars = () if picks is None else (picks,)
    return pl.pallas_call(
        kernel,
        out_shape=tuple(jax.ShapeDtypeStruct(shape, jnp.bfloat16) for shape in shapes),
        grid_spec=pltpu.PrefetchScalarGridSpec(
            num_scalar_prefetch=len(scalars),
            grid=(),
            in_specs=[ANY] * len(arrays),
            out_specs=tuple(pl.BlockSpec(memory_space=pltpu.VMEM) for _ in shapes),
            scratch_shapes=[pltpu.SemaphoreType.DMA((ncopies,))],
        ),
        cost_estimate=pl.CostEstimate(flops=0, bytes_accessed=6000000, transcendentals=0),
    )(*scalars, *arrays)


def tables(rand_blocks, global_ids, me, nblocks, nctx):
    my_y, my_z = me // NZ, me % NZ
    requests = rand_blocks.reshape(nctx, nblocks * 3)
    mine = lax.dynamic_index_in_dim(requests, me, 0, keepdims=False)
    pairs = [(i, 1, -2) for i in range(4)] + [(0, 2, -2), (1, 2, -2)]
    pairs += [(i, -1, 2) for i in range(4)] + [(2, -2, 2), (3, -2, 2)]
    for row in (1, 2, 3):
        pairs += [(row, 0, d) for d in (0, -1, 1, -2, 2)]
    offsets = jnp.array(pairs, jnp.int32)
    consumer = ((my_y + offsets[:, 0]) & (NY - 1)) * NZ + ((my_z + offsets[:, 1]) & (NZ - 1))
    source = my_y * NZ + ((my_z + offsets[:, 2]) & (NZ - 1))
    shift = nblocks.bit_length() - 1
    wanted = requests[consumer]
    picks = jnp.sum(
        jnp.where((wanted >> shift) == source[:, None], wanted & (nblocks - 1), 0), axis=1
    )
    g_shard = global_ids >> shift
    g_y, g_z = g_shard >> 3, g_shard & (NZ - 1)
    arange4 = jnp.arange(NY)
    picks = jnp.concatenate(
        [
            picks,
            global_ids & (nblocks - 1),
            ((my_y + arange4) & (NY - 1)) * (BS // NY),
            (my_y - g_y) & (NY - 1),
            (my_z - g_z) & (NZ - 1),
        ]
    ).astype(jnp.int32)
    src = mine >> shift
    inside = mine & (nblocks - 1)
    dy = ((src >> 3) - my_y) & (NY - 1)
    dz = (my_z - src) & (NZ - 1)
    late = (dz >= 3) & (dz <= 5)
    near_slot = jnp.where(late, 0, inside)
    order = jnp.where(
        late, jnp.where(dz == 3, 0, jnp.where(dz == 5, 1, 2)),
        jnp.where(dz == 0, 0, jnp.where(dz == 1, 1, jnp.where(dz == 7, 2, jnp.where(dz == 2, 3, 4)))),
    )
    row = jnp.where(dy == 1, 1, jnp.where(dy == 2, 2, 0))
    second = (dz == 2) | (dz == 6)
    block = jnp.arange(nblocks)
    edges = jnp.stack([me == 0, me == nctx - 1]).astype(jnp.int32)
    piece_rows = ((my_y - arange4) & (NY - 1)) * (BS // NY)
    codes = []
    for chunk in range(2):
        edge_slot = chunk * 4 + 3
        far = jnp.where(late, LYP, jnp.where(second, MP, YP)) + row
        base = jnp.where(late, 0, jnp.where(second, chunk * 2 - 3, chunk * jnp.where(row == 2, 3, 4)))
        rand_code = jnp.where(dy == 0, dz * 8 + near_slot, far * 8 + order + base).reshape(nblocks, 3)
        left = jnp.where(
            block == 0, jnp.where(my_z == 0, YP * 8 + edge_slot, L1 * 8 + nblocks - 1), block - 1
        )
        right = jnp.where(
            block == nblocks - 1, jnp.where(my_z == NZ - 1, YM * 8 + edge_slot, R1 * 8), block + 1
        )
        listed = jnp.concatenate([jnp.stack([left, block, right], axis=1), rand_code], axis=1)
        codes.append(jnp.concatenate([listed.reshape(-1), edges, piece_rows]).astype(jnp.int32))
    return picks, codes


def whole_step(queries, key_value, lanczos_vec, rand_blocks, global_ids):
    rows, width = queries.shape
    nblocks = rows // BS
    nctx = lax.axis_size("ctx")
    nhead = lax.axis_size("head")
    me = lax.axis_index("ctx")
    picks, codes = tables(rand_blocks, global_ids, me, nblocks, nctx)
    blocks = key_value.reshape(2, nblocks, BS, width)
    piece = (2, 2, BS // NY, width)
    quarters = pack(split_kernel, picks, (blocks,), (piece,) * NY, 8)
    held = (
        quarters[0],
        send(quarters[1], y_shift(1)),
        send(quarters[2], y_shift(2)),
        send(quarters[3], y_shift(-1)),
    )
    (mine,) = pack(functools.partial(choose_kernel, 33), picks, held, (piece,), 2)
    from_left = send(mine, z_shift(1))
    from_right = send(mine, z_shift(-1))
    (close,) = pack(
        functools.partial(choose_kernel, 35), picks,
        (mine, from_left, mine, mine, mine, mine, mine, from_right), (piece,), 2,
    )
    hop_left = send(close, z_shift(3))
    hop_right = send(close, z_shift(-3))
    (quarter,) = pack(
        functools.partial(choose_kernel, 35), picks,
        (close, close, hop_left, hop_left, hop_left, hop_right, hop_right, close), (piece,), 2,
    )
    pieces = (
        quarter, send(quarter, y_shift(1)), send(quarter, y_shift(2)), send(quarter, y_shift(-1))
    )
    cw = CHUNKS[0][1] * HD

    def slots(count):
        return (count, 2, BS, cw)

    def rows_of(packed):
        return tuple(send(x, y_shift(d)) for x, d in zip(packed, (1, 2, -1)))

    own, l1, r1, l2, r2 = [], [], [], [], []
    for k, (first, heads) in enumerate(CHUNKS):
        own.append(jnp.swapaxes(blocks[..., first * HD : (first + heads) * HD], 0, 1))
        l1.append(send(own[k], z_shift(1)))
        r1.append(send(own[k], z_shift(-1)))
        l2.append(send(l1[k], z_shift(1)))
        r2.append(send(r1[k], z_shift(-1)))
    y1 = rows_of(
        pack(
            first_kernel, picks, (own[0], l1[0], r1[0], own[1], l1[1], r1[1]),
            (slots(8), slots(6), slots(8)), 22,
        ),
    )
    plus, minus = pack(third_kernel, picks, (l2[0], r2[0]), (slots(6), slots(6)), 12)
    a3, b3 = send(plus, z_shift(1)), send(minus, z_shift(-1))
    plus, minus, *two = pack(
        second_kernel, picks, (l2[0], r2[0], l2[1], r2[1]),
        (slots(6), slots(6)) + (slots(4),) * 3, 24,
    )
    y2 = rows_of(two)
    c3, d3 = send(plus, z_shift(1)), send(minus, z_shift(-1))
    a4, b4 = send(a3[4:6], z_shift(1)), send(b3[4:6], z_shift(-1))
    c4, d4 = send(c3[4:6], z_shift(1)), send(d3[4:6], z_shift(-1))
    y3a = rows_of(pack(late_kernel, None, (a3, b3, a4, b4), (slots(3),) * 3, 9))
    y3b = rows_of(pack(late_kernel, None, (c3, d3, c4, d4), (slots(3),) * 3, 9))

    def by_code(y):
        return (y[0], y[2], y[1])

    sources = (
        (own[0], l1[0], l2[0], a3, a4, b3, r2[0], r1[0]) + by_code(y1) + by_code(y3a) + by_code(y2),
        (own[1], l1[1], l2[1], c3, c4, d3, r2[1], r1[1]) + by_code(y1) + by_code(y3b) + by_code(y2),
    )
    products = []
    stats = []
    keys = LIST * BS
    for k, arrays in enumerate(sources):
        product, stat = pl.pallas_call(
            functools.partial(attention_kernel, nblocks, (CHUNKS[k][0], k), len(arrays)),
            out_shape=(
                jax.ShapeDtypeStruct((rows, cw), jnp.float32),
                jax.ShapeDtypeStruct((8, 128), jnp.float32),
            ),
            grid_spec=pltpu.PrefetchScalarGridSpec(
                num_scalar_prefetch=1,
                grid=(nblocks,),
                in_specs=[pl.BlockSpec((BS, cw), lambda b, *_, k=k: (b, k))] * 2
                + [ANY] * (len(arrays) + NY),
                out_specs=(
                    pl.BlockSpec((BS, cw), lambda b, *_: (b, 0)),
                    pl.BlockSpec((8, 128), lambda b, *_: (0, 0)),
                ),
                scratch_shapes=[
                    pltpu.VMEM((2, 2, keys, cw), jnp.bfloat16),
                    pltpu.SemaphoreType.DMA((2, 2 * LIST)),
                    pltpu.VMEM((nblocks, 8, cw), jnp.float32),
                ],
            ),
            cost_estimate=pl.CostEstimate(
                flops=10 * rows * keys * cw, bytes_accessed=16 * rows * cw,
                transcendentals=rows * keys * (cw // HD),
            ),
        )(codes[k], queries, lanczos_vec, *arrays, *pieces)
        products.append(product)
        stats.append(stat)
    sent = jnp.broadcast_to(sum(stats)[:1], (nctx * nhead, 128))
    gathered = lax.all_to_all(sent, ("ctx", "head"), 0, 0, tiled=True)
    count = float(rows * width * nctx * nhead)
    step = rows // 4
    fin_spec = pl.BlockSpec((step, width), lambda i: (i, 0))
    part_specs = [pl.BlockSpec((step, heads * HD), lambda i: (i, 0)) for _, heads in CHUNKS]
    next_vec, coef = pl.pallas_call(
        functools.partial(finish_kernel, count),
        out_shape=(
            jax.ShapeDtypeStruct((rows, width), jnp.float32),
            jax.ShapeDtypeStruct((8, 128), jnp.float32),
        ),
        grid=(4,),
        in_specs=[pl.BlockSpec((nctx * nhead, 128), lambda i: (0, 0))] + part_specs + [fin_spec],
        out_specs=(fin_spec, pl.BlockSpec((8, 128), lambda i: (0, 0))),
        scratch_shapes=[pltpu.VMEM((8, 128), jnp.float32)],
        name="finish",
    )(gathered, *products, lanczos_vec)
    return next_vec, coef[0, :2]


def solution(mesh):
    placed = (P("ctx", "head"), P(None, "ctx", "head"), P("ctx", "head"), P(), P())
    return jax.shard_map(
        whole_step, mesh=mesh, in_specs=placed, out_specs=(P("ctx", "head"), P()), check_vma=False
    )
```

```python
import functools

import jax
import jax.numpy as jnp
from jax import lax
from jax.experimental import pallas as pl
from jax.experimental.pallas import tpu as pltpu
from jax.sharding import PartitionSpec as P


HD = 128
BS = 128
LIST = 8
SCALE = HD ** (-0.5)
LOG2E = 1.4426950408889634
NT = (((1,), (1,)), ((), ()))


def attend_tiles(tiles, left_bias, right_bias):
    count = range(len(tiles))
    logits = [
        lax.dot_general(
            jnp.concatenate([q, tangent], axis=0), keys, NT, preferred_element_type=jnp.float32
        )
        for q, tangent, keys, _ in tiles
    ]
    prob, dots = [], []
    for x in logits:
        scores = x[:BS]
        scores = jnp.concatenate(
            [
                scores[:, :BS] + left_bias,
                scores[:, BS : 2 * BS],
                scores[:, 2 * BS : 3 * BS] + right_bias,
                scores[:, 3 * BS :],
            ],
            axis=1,
        )
        row_top = jnp.max(scores, axis=1, keepdims=True)
        weights = jnp.exp2((scores - row_top) * (SCALE * LOG2E))
        prob.append(weights * (1.0 / jnp.sum(weights, axis=1, keepdims=True)))
        dots.append(x[BS:])
    dout = []
    for i in count:
        center = jnp.sum(prob[i] * dots[i], axis=1, keepdims=True)
        first = ((prob[i] * SCALE) * (dots[i] - center)).astype(jnp.bfloat16)
        dout.append(jnp.dot(first, tiles[i][3], preferred_element_type=jnp.float32).astype(jnp.bfloat16))
    dprob = [
        lax.dot_general(dout[i], tiles[i][3], NT, preferred_element_type=jnp.float32) for i in count
    ]
    out = []
    for i in count:
        center = jnp.sum(prob[i] * dprob[i], axis=1, keepdims=True)
        second = (prob[i] * (dprob[i] - center)).astype(jnp.bfloat16)
        out.append(jnp.dot(second, tiles[i][2], preferred_element_type=jnp.float32) * SCALE)
    return out


NY, NZ = 4, 8
CHUNKS = ((0, 2), (2, 2))
CALLS = len(CHUNKS)
OWN, L1, _, _, _, _, _, R1, YP, YM, _, LYP, _, _, MP, MM, M2, FP, _, _ = range(20)


def start_choice(arrays, ids, code, dst, sem):
    which = lax.shift_right_logical(code, 3)
    slot = code & 7
    for k in ids:
        @pl.when(which == k)
        def _(k=k):
            pltpu.make_async_copy(arrays[k].at[slot], dst, sem).start()


def attention_kernel(nblocks, chunk, narrays, code_ref, q_ref, vec_ref, *refs):
    arrays = refs[:narrays]
    quarter = refs[narrays]
    out_ref, stat_ref, kvbuf, sems, acc = refs[narrays + 1 :]
    b = pl.program_id(0)
    width = q_ref.shape[1]
    table = nblocks * 6
    listed = (0, 1, 2, 5, 6, 7)

    def place(slot, pos):
        return kvbuf.at[slot, :, pl.ds(pos * BS, BS)]

    def globals_in(slot):
        copies = []
        cols = pl.ds(chunk[0] * HD, width)
        part = BS // NY
        for i, array in enumerate((None, MP, M2, MM)):
            rows = pl.multiple_of(code_ref[table + 2 + i], BS // NY)
            for g in range(2):
                dst = kvbuf.at[slot, :, pl.ds((3 + g) * BS + rows, BS // NY)]
                sem = sems.at[slot, LIST + 2 * i + g]
                if array is None:
                    src = quarter.at[g, :, :, cols]
                else:
                    src = arrays[array].at[4, :, pl.ds((2 * g + chunk[1]) * part, part)]
                copies.append(pltpu.make_async_copy(src, dst, sem))
        return copies

    def start(blk, slot):
        for j, pos in enumerate(listed):
            ids = (
                (OWN, L1, YP) if pos == 0 else (OWN,) if pos == 1 else (OWN, R1, YM) if pos == 2
                else tuple(range(narrays))
            )
            start_choice(arrays, ids, code_ref[blk * 6 + j], place(slot, pos), sems.at[slot, pos])

        @pl.when(blk < 2)
        def _():
            for cp in globals_in(slot):
                cp.start()

    slot = lax.rem(b, 2)

    @pl.when(b == 0)
    def _():
        start(0, 0)

    @pl.when(b + 1 < nblocks)
    def _():
        start(b + 1, 1 - slot)

    for pos in listed:
        pltpu.make_async_copy(arrays[OWN].at[0], place(slot, pos), sems.at[slot, pos]).wait()

    @pl.when(b < 2)
    def _():
        for cp in globals_in(slot):
            cp.wait()

    left_bias = jnp.where((b == 0) & (code_ref[table] == 1), -1e30, 0.0).astype(jnp.float32)
    right_bias = jnp.where((b == nblocks - 1) & (code_ref[table + 1] == 1), -1e30, 0.0).astype(jnp.float32)
    heads = [slice(h * HD, (h + 1) * HD) for h in range(width // HD)]
    tiles = [
        (
            q_ref[:, cols], vec_ref[:, cols].astype(jnp.bfloat16),
            kvbuf[slot, 0, :, cols], kvbuf[slot, 1, :, cols],
        )
        for cols in heads
    ]
    for cols, prod in zip(heads, attend_tiles(tiles, left_bias, right_bias)):
        vec = vec_ref[:, cols]
        out_ref[:, cols] = prod
        s = jnp.sum(vec * vec, axis=0, keepdims=True)
        c = jnp.sum(vec * prod, axis=0, keepdims=True)
        a = jnp.where(s > 0, c / jnp.where(s > 0, s, 1.0), 0.0)
        d = prod - a * vec
        acc[b, 0:1, cols] = s
        acc[b, 1:2, cols] = c
        acc[b, 2:3, cols] = jnp.sum(d * d, axis=0, keepdims=True)

    @pl.when(b == nblocks - 1)
    def _():
        s, c, r = combine(acc[:, 0, :], acc[:, 1, :], acc[:, 2, :])
        lane = lax.broadcasted_iota(jnp.int32, stat_ref.shape, 1) - 3 * chunk[1]
        stat_ref[...] = jnp.where(lane == 0, s, jnp.where(lane == 1, c, jnp.where(lane == 2, r, 0.0)))


def run_copies(plan, sems):
    copies = [pltpu.make_async_copy(src, dst, sems.at[i]) for i, (src, dst) in enumerate(plan)]
    for cp in copies:
        cp.start()
    for cp in copies:
        cp.wait()


def first_kernel(pick_ref, own_a, l1_a, r1_a, own_b, l1_b, r1_b, yp, y2, ym, sems):
    plan = []
    for k, arrays in enumerate(((own_a, l1_a, r1_a), (own_b, l1_b, r1_b))):
        for row, (out, step) in enumerate(((yp, 4), (y2, 3), (ym, 4))):
            for i, src in enumerate(arrays):
                plan.append((src.at[pick_ref[12 + row * 5 + i]], out.at[k * step + i]))
        plan.append((arrays[1].at[own_a.shape[0] - 1], yp.at[k * 4 + 3]))
        plan.append((arrays[2].at[0], ym.at[k * 4 + 3]))
    run_copies(plan, sems)


def third_hop(pick_ref, l2, r2, plus, minus):
    plan = []
    for i in range(6):
        plan.append((l2.at[pick_ref[i]], plus.at[i]))
        plan.append((r2.at[pick_ref[6 + i]], minus.at[i]))
    return plan


def third_kernel(pick_ref, l2, r2, plus, minus, sems):
    run_copies(third_hop(pick_ref, l2, r2, plus, minus), sems)


def second_kernel(pick_ref, l2_a, r2_a, l2_b, r2_b, quarter, plus, minus, yp, y2, ym, sems):
    plan = third_hop(pick_ref, l2_b, r2_b, plus, minus)
    for row, out in enumerate((yp, y2, ym)):
        for i, src in enumerate((l2_a, r2_a, l2_b, r2_b)):
            plan.append((src.at[pick_ref[12 + row * 5 + 3 + i % 2]], out.at[i]))
        part, half = quarter.shape[2], quarter.shape[3] // 2
        for g in range(2):
            for k in range(2):
                plan.append(
                    (
                        quarter.at[g, :, :, pl.ds(k * half, half)],
                        out.at[4, :, pl.ds((2 * g + k) * part, part)],
                    )
                )
    run_copies(plan, sems)


def half_kernel(a3, b3, yp, y2, ym, sems):
    plan = []
    for row, out in enumerate((yp, y2, ym)):
        plan += [(a3.at[row + 1], out.at[0]), (b3.at[row + 1], out.at[1])]
    run_copies(plan, sems)


def late_kernel(a3, b3, a4, b4, yp, y2, ym, sems):
    last = (a4.at[1], b4.at[0], b4.at[1])
    plan = []
    for row, out in enumerate((yp, y2, ym)):
        plan += [(a3.at[row + 1], out.at[0]), (b3.at[row + 1], out.at[1]), (last[row], out.at[2])]
    run_copies(plan, sems)


def split_kernel(pick_ref, blocks, p0, p1, p2, p3, sems):
    plan = []
    for i, out in enumerate((p0, p1, p2, p3)):
        rows = pl.ds(pl.multiple_of(pick_ref[29 + i], BS // NY), BS // NY)
        for g in range(2):
            plan.append((blocks.at[:, pick_ref[27 + g], rows], out.at[g]))
    run_copies(plan, sems)


def choose_kernel(at, pick_ref, *refs):
    srcs, out, sems = refs[:-2], refs[-2], refs[-1]
    for g in range(2):
        for k, src in enumerate(srcs):
            @pl.when(pick_ref[at + g] == k)
            def _(src=src, g=g):
                pltpu.make_async_copy(src.at[g], out.at[g], sems.at[g]).start()
    for g in range(2):
        pltpu.make_async_copy(srcs[0].at[g], out.at[g], sems.at[g]).wait()


def total(x):
    return jnp.sum(jnp.sum(x, axis=0, keepdims=True), axis=1, keepdims=True)


def combine(s, c, r):
    s_all = total(s)
    c_all = total(c)
    a = jnp.where(s > 0, c / jnp.where(s > 0, s, 1.0), 0.0)
    a_all = jnp.where(s_all > 0, c_all / jnp.where(s_all > 0, s_all, 1.0), 0.0)
    gap = a - a_all
    return s_all, c_all, total(r + (s * gap) * gap)


def finish_kernel(count, gathered, *refs):
    prods = refs[:CALLS]
    vec_ref, out_ref, coef_ref, ab = refs[CALLS:]
    step = pl.program_id(0)

    @pl.when(step == 0)
    def _():
        table = gathered[...]
        parts = [[table[:, 3 * k + i : 3 * k + i + 1] for i in range(3)] for k in range(CALLS)]
        alpha = sum(total(c) for _, c, _ in parts) * (1.0 / count)
        square = 0.0
        for s, c, r in parts:
            gap = jnp.where(s > 0, c / jnp.where(s > 0, s, 1.0), 0.0) - alpha
            square = square + total(r + (s * gap) * gap)
        beta = jnp.sqrt(square * (1.0 / count) + 1e-06)
        ab[0:1, :] = jnp.broadcast_to(alpha, (1, 128))
        ab[1:2, :] = jnp.broadcast_to(1.0 / beta, (1, 128))
        coef_ref[0] = alpha[0, 0]
        coef_ref[1] = beta[0, 0]

    alpha = ab[0:1, 0:1]
    inv = ab[1:2, 0:1]
    for (first, heads), prod in zip(CHUNKS, prods):
        cols = slice(first * HD, (first + heads) * HD)
        out_ref[:, cols] = (prod[...] - alpha * vec_ref[:, cols]) * inv


def z_shift(d):
    return [(y * NZ + z, y * NZ + (z + d) % NZ) for y in range(NY) for z in range(NZ)]


def y_shift(d):
    return [(y * NZ + z, (y + d) % NY * NZ + z) for y in range(NY) for z in range(NZ)]


def send(x, pairs):
    return lax.ppermute(x, "ctx", pairs)


ANY = pl.BlockSpec(memory_space=pltpu.HBM)


def pack(kernel, picks, arrays, shapes, ncopies):
    scalars = () if picks is None else (picks,)
    return pl.pallas_call(
        kernel,
        out_shape=tuple(jax.ShapeDtypeStruct(shape, jnp.bfloat16) for shape in shapes),
        grid_spec=pltpu.PrefetchScalarGridSpec(
            num_scalar_prefetch=len(scalars),
            grid=(),
            in_specs=[ANY] * len(arrays),
            out_specs=tuple(pl.BlockSpec(memory_space=pltpu.VMEM) for _ in shapes),
            scratch_shapes=[pltpu.SemaphoreType.DMA((ncopies,))],
        ),
        cost_estimate=pl.CostEstimate(flops=0, bytes_accessed=6000000, transcendentals=0),
    )(*scalars, *arrays)


def tables(rand_blocks, global_ids, me, nblocks, nctx):
    my_y, my_z = me // NZ, me % NZ
    requests = rand_blocks.reshape(nctx, nblocks * 3)
    mine = lax.dynamic_index_in_dim(requests, me, 0, keepdims=False)
    pairs = [(i, 1, -2) for i in range(4)] + [(0, 2, -2), (1, 2, -2)]
    pairs += [(i, -1, 2) for i in range(4)] + [(2, -2, 2), (3, -2, 2)]
    for row in (1, 2, 3):
        pairs += [(row, 0, d) for d in (0, -1, 1, -2, 2)]
    offsets = jnp.array(pairs, jnp.int32)
    consumer = ((my_y + offsets[:, 0]) & (NY - 1)) * NZ + ((my_z + offsets[:, 1]) & (NZ - 1))
    source = my_y * NZ + ((my_z + offsets[:, 2]) & (NZ - 1))
    shift = nblocks.bit_length() - 1
    wanted = requests[consumer]
    picks = jnp.sum(
        jnp.where((wanted >> shift) == source[:, None], wanted & (nblocks - 1), 0), axis=1
    )
    g_shard = global_ids >> shift
    g_y, g_z = g_shard >> 3, g_shard & (NZ - 1)
    arange4 = jnp.arange(NY)
    picks = jnp.concatenate(
        [
            picks,
            global_ids & (nblocks - 1),
            ((my_y + arange4) & (NY - 1)) * (BS // NY),
            (my_y - g_y) & (NY - 1),
            (my_z - g_z) & (NZ - 1),
        ]
    ).astype(jnp.int32)
    src = mine >> shift
    inside = mine & (nblocks - 1)
    dy = ((src >> 3) - my_y) & (NY - 1)
    dz = (my_z - src) & (NZ - 1)
    late = (dz >= 3) & (dz <= 5)
    near_slot = jnp.where(late, 0, inside)
    order = jnp.where(
        late, jnp.where(dz == 3, 0, jnp.where(dz == 5, 1, 2)),
        jnp.where(dz == 0, 0, jnp.where(dz == 1, 1, jnp.where(dz == 7, 2, jnp.where(dz == 2, 3, 4)))),
    )
    row = jnp.where(dy == 1, 1, jnp.where(dy == 2, 2, 0))
    second = (dz == 2) | (dz == 6)
    block = jnp.arange(nblocks)
    edges = jnp.stack([me == 0, me == nctx - 1]).astype(jnp.int32)
    piece_rows = ((my_y - arange4) & (NY - 1)) * (BS // NY)
    codes = []
    for chunk in range(2):
        edge_slot = chunk * 4 + 3
        far = jnp.where(late, LYP, jnp.where(second, MP, YP)) + row
        base = jnp.where(late, 0, jnp.where(second, chunk * 2 - 3, chunk * jnp.where(row == 2, 3, 4)))
        if chunk == 0:
            far = jnp.where(dz == 4, FP + row, far)
            base = jnp.where(dz == 4, -2, base)
        rand_code = jnp.where(dy == 0, dz * 8 + near_slot, far * 8 + order + base).reshape(nblocks, 3)
        left = jnp.where(
            block == 0, jnp.where(my_z == 0, YP * 8 + edge_slot, L1 * 8 + nblocks - 1), block - 1
        )
        right = jnp.where(
            block == nblocks - 1, jnp.where(my_z == NZ - 1, YM * 8 + edge_slot, R1 * 8), block + 1
        )
        listed = jnp.concatenate([jnp.stack([left, block, right], axis=1), rand_code], axis=1)
        codes.append(jnp.concatenate([listed.reshape(-1), edges, piece_rows]).astype(jnp.int32))
    return picks, codes


def whole_step(queries, key_value, lanczos_vec, rand_blocks, global_ids):
    rows, width = queries.shape
    nblocks = rows // BS
    nctx = lax.axis_size("ctx")
    nhead = lax.axis_size("head")
    me = lax.axis_index("ctx")
    picks, codes = tables(rand_blocks, global_ids, me, nblocks, nctx)
    blocks = key_value.reshape(2, nblocks, BS, width)
    piece = (2, 2, BS // NY, width)
    quarters = pack(split_kernel, picks, (blocks,), (piece,) * NY, 8)
    held = (
        quarters[0],
        send(quarters[1], y_shift(1)),
        send(quarters[2], y_shift(2)),
        send(quarters[3], y_shift(-1)),
    )
    (mine,) = pack(functools.partial(choose_kernel, 33), picks, held, (piece,), 2)
    from_left = send(mine, z_shift(1))
    from_right = send(mine, z_shift(-1))
    (close,) = pack(
        functools.partial(choose_kernel, 35), picks,
        (mine, from_left, mine, mine, mine, mine, mine, from_right), (piece,), 2,
    )
    hop_left = send(close, z_shift(3))
    hop_right = send(close, z_shift(-3))
    (quarter,) = pack(
        functools.partial(choose_kernel, 35), picks,
        (close, close, hop_left, hop_left, hop_left, hop_right, hop_right, close), (piece,), 2,
    )
    cw = CHUNKS[0][1] * HD

    def slots(count):
        return (count, 2, BS, cw)

    def rows_of(packed):
        return tuple(send(x, y_shift(d)) for x, d in zip(packed, (1, 2, -1)))

    own, l1, r1, l2, r2 = [], [], [], [], []
    for k, (first, heads) in enumerate(CHUNKS):
        own.append(jnp.swapaxes(blocks[..., first * HD : (first + heads) * HD], 0, 1))
        l1.append(send(own[k], z_shift(1)))
        r1.append(send(own[k], z_shift(-1)))
        l2.append(send(l1[k], z_shift(1)))
        r2.append(send(r1[k], z_shift(-1)))
    y1 = rows_of(
        pack(
            first_kernel, picks, (own[0], l1[0], r1[0], own[1], l1[1], r1[1]),
            (slots(8), slots(6), slots(8)), 22,
        ),
    )
    plus, minus = pack(third_kernel, picks, (l2[0], r2[0]), (slots(6), slots(6)), 12)
    a3, b3 = send(plus, z_shift(1)), send(minus, z_shift(-1))
    plus, minus, *two = pack(
        second_kernel, picks, (l2[0], r2[0], l2[1], r2[1], quarter),
        (slots(6), slots(6)) + (slots(5),) * 3, 36,
    )
    y2 = rows_of(two)
    c3, d3 = send(plus, z_shift(1)), send(minus, z_shift(-1))
    a4, b4 = send(a3[4:6], z_shift(1)), send(b3[4:6], z_shift(-1))
    c4, d4 = send(c3[4:6], z_shift(1)), send(d3[4:6], z_shift(-1))
    y3a = rows_of(pack(half_kernel, None, (a3, b3), (slots(2),) * 3, 6))
    y4a = rows_of((a4[1:2], b4[0:1], b4[1:2]))
    y3b = rows_of(pack(late_kernel, None, (c3, d3, c4, d4), (slots(3),) * 3, 9))

    def by_code(y):
        return (y[0], y[2], y[1])

    sources = (
        (own[0], l1[0], l2[0], a3, a4, b3, r2[0], r1[0]) + by_code(y1) + by_code(y3a) + by_code(y2)
        + by_code(y4a),
        (own[1], l1[1], l2[1], c3, c4, d3, r2[1], r1[1]) + by_code(y1) + by_code(y3b) + by_code(y2),
    )
    products = []
    stats = []
    keys = LIST * BS
    for k, arrays in enumerate(sources):
        product, stat = pl.pallas_call(
            functools.partial(attention_kernel, nblocks, (CHUNKS[k][0], k), len(arrays)),
            out_shape=(
                jax.ShapeDtypeStruct((rows, cw), jnp.float32),
                jax.ShapeDtypeStruct((8, 128), jnp.float32),
            ),
            grid_spec=pltpu.PrefetchScalarGridSpec(
                num_scalar_prefetch=1,
                grid=(nblocks,),
                in_specs=[pl.BlockSpec((BS, cw), lambda b, *_, k=k: (b, k))] * 2
                + [ANY] * (len(arrays) + 1),
                out_specs=(
                    pl.BlockSpec((BS, cw), lambda b, *_: (b, 0)),
                    pl.BlockSpec((8, 128), lambda b, *_: (0, 0)),
                ),
                scratch_shapes=[
                    pltpu.VMEM((2, 2, keys, cw), jnp.bfloat16),
                    pltpu.SemaphoreType.DMA((2, 2 * LIST)),
                    pltpu.VMEM((nblocks, 8, cw), jnp.float32),
                ],
            ),
            cost_estimate=pl.CostEstimate(
                flops=10 * rows * keys * cw, bytes_accessed=16 * rows * cw,
                transcendentals=rows * keys * (cw // HD),
            ),
        )(codes[k], queries, lanczos_vec, *arrays, quarter)
        products.append(product)
        stats.append(stat)
    sent = jnp.broadcast_to(sum(stats)[:1], (nctx * nhead, 128))
    gathered = lax.all_to_all(sent, ("ctx", "head"), 0, 0, tiled=True)
    count = float(rows * width * nctx * nhead)
    step = rows // 4
    fin_spec = pl.BlockSpec((step, width), lambda i: (i, 0))
    part_specs = [pl.BlockSpec((step, heads * HD), lambda i: (i, 0)) for _, heads in CHUNKS]
    next_vec, coef = pl.pallas_call(
        functools.partial(finish_kernel, count),
        out_shape=(
            jax.ShapeDtypeStruct((rows, width), jnp.float32),
            jax.ShapeDtypeStruct((2,), jnp.float32),
        ),
        grid=(4,),
        in_specs=[pl.BlockSpec((nctx * nhead, 128), lambda i: (0, 0))] + part_specs + [fin_spec],
        out_specs=(fin_spec, pl.BlockSpec(memory_space=pltpu.SMEM)),
        scratch_shapes=[pltpu.VMEM((8, 128), jnp.float32)],
        name="finish",
    )(gathered, *products, lanczos_vec)
    return next_vec, coef


def solution(mesh):
    placed = (P("ctx", "head"), P(None, "ctx", "head"), P("ctx", "head"), P(), P())
    return jax.shard_map(
        whole_step, mesh=mesh, in_specs=placed, out_specs=(P("ctx", "head"), P()), check_vma=False
    )
```

```python
import functools

import jax
import jax.numpy as jnp
from jax import lax
from jax.experimental import pallas as pl
from jax.experimental.pallas import tpu as pltpu
from jax.sharding import PartitionSpec as P


HD = 128
BS = 128
LIST = 8
SCALE = HD ** (-0.5)
LOG2E = 1.4426950408889634
NT = (((1,), (1,)), ((), ()))


def attend_tiles(tiles, left_bias, right_bias):
    count = range(len(tiles))
    logits = [
        lax.dot_general(
            jnp.concatenate([q, tangent], axis=0), keys, NT, preferred_element_type=jnp.float32
        )
        for q, tangent, keys, _ in tiles
    ]
    prob, dots = [], []
    for x in logits:
        scores = x[:BS]
        scores = jnp.concatenate(
            [
                scores[:, :BS] + left_bias,
                scores[:, BS : 2 * BS],
                scores[:, 2 * BS : 3 * BS] + right_bias,
                scores[:, 3 * BS :],
            ],
            axis=1,
        )
        row_top = jnp.max(scores, axis=1, keepdims=True)
        weights = jnp.exp2((scores - row_top) * (SCALE * LOG2E))
        prob.append(weights * (1.0 / jnp.sum(weights, axis=1, keepdims=True)))
        dots.append(x[BS:])
    dout = []
    for i in count:
        center = jnp.sum(prob[i] * dots[i], axis=1, keepdims=True)
        first = ((prob[i] * SCALE) * (dots[i] - center)).astype(jnp.bfloat16)
        dout.append(jnp.dot(first, tiles[i][3], preferred_element_type=jnp.float32).astype(jnp.bfloat16))
    dprob = [
        lax.dot_general(dout[i], tiles[i][3], NT, preferred_element_type=jnp.float32) for i in count
    ]
    out = []
    for i in count:
        center = jnp.sum(prob[i] * dprob[i], axis=1, keepdims=True)
        second = (prob[i] * (dprob[i] - center)).astype(jnp.bfloat16)
        out.append(jnp.dot(second, tiles[i][2], preferred_element_type=jnp.float32) * SCALE)
    return out


NY, NZ = 4, 8
CHUNKS = ((0, 2), (2, 2))
CALLS = len(CHUNKS)
OWN, L1, _, _, _, _, _, R1, YP, YM, _, LYP, _, _, MP, MM, M2, FP, _, _ = range(20)


def start_choice(arrays, ids, code, dst, sem):
    which = lax.shift_right_logical(code, 3)
    slot = code & 7

    def search(options):
        if len(options) == 1:
            pltpu.make_async_copy(arrays[options[0]].at[slot], dst, sem).start()
            return
        half = len(options) // 2
        lax.cond(
            which < options[half], lambda: search(options[:half]), lambda: search(options[half:])
        )

    search(sorted(ids))


def attention_kernel(nblocks, chunk, narrays, code_ref, q_ref, vec_ref, *refs):
    arrays = refs[:narrays]
    quarter = refs[narrays]
    before = refs[narrays + 1 : -5]
    out_ref, stat_ref, kvbuf, sems, acc = refs[-5:]
    b = pl.program_id(0)
    width = q_ref.shape[1]
    table = nblocks * 6
    listed = (0, 1, 2, 5, 6, 7)

    def place(slot, pos):
        return kvbuf.at[slot, :, pl.ds(pos * BS, BS)]

    def globals_in(slot):
        copies = []
        cols = pl.ds(chunk[0] * HD, width)
        part = BS // NY
        for i, array in enumerate((None, MP, M2, MM)):
            rows = pl.multiple_of(code_ref[table + 2 + i], BS // NY)
            for g in range(2):
                dst = kvbuf.at[slot, :, pl.ds((3 + g) * BS + rows, BS // NY)]
                sem = sems.at[slot, LIST + 2 * i + g]
                if array is None:
                    src = quarter.at[g, :, :, cols]
                else:
                    src = arrays[array].at[2, :, pl.ds((2 * g + chunk[1]) * part, part)]
                copies.append(pltpu.make_async_copy(src, dst, sem))
        return copies

    def start(blk, slot):
        for j, pos in enumerate(listed):
            ids = (
                (OWN, L1, YP) if pos == 0 else (OWN,) if pos == 1 else (OWN, R1, YM) if pos == 2
                else tuple(range(narrays))
            )
            start_choice(arrays, ids, code_ref[blk * 6 + j], place(slot, pos), sems.at[slot, pos])

        @pl.when(blk < 2)
        def _():
            for cp in globals_in(slot):
                cp.start()

    slot = lax.rem(b, 2)

    @pl.when(b == 0)
    def _():
        start(0, 0)

    @pl.when(b + 1 < nblocks)
    def _():
        start(b + 1, 1 - slot)

    for pos in listed:
        pltpu.make_async_copy(arrays[OWN].at[0], place(slot, pos), sems.at[slot, pos]).wait()

    @pl.when(b < 2)
    def _():
        for cp in globals_in(slot):
            cp.wait()

    left_bias = jnp.where((b == 0) & (code_ref[table] == 1), -1e30, 0.0).astype(jnp.float32)
    right_bias = jnp.where((b == nblocks - 1) & (code_ref[table + 1] == 1), -1e30, 0.0).astype(jnp.float32)
    heads = [slice(h * HD, (h + 1) * HD) for h in range(width // HD)]
    tiles = [
        (
            q_ref[:, cols], vec_ref[:, cols].astype(jnp.bfloat16),
            kvbuf[slot, 0, :, cols], kvbuf[slot, 1, :, cols],
        )
        for cols in heads
    ]
    for cols, prod in zip(heads, attend_tiles(tiles, left_bias, right_bias)):
        vec = vec_ref[:, cols]
        out_ref[:, cols] = prod
        s = jnp.sum(vec * vec, axis=0, keepdims=True)
        c = jnp.sum(vec * prod, axis=0, keepdims=True)
        a = jnp.where(s > 0, c / jnp.where(s > 0, s, 1.0), 0.0)
        d = prod - a * vec
        acc[b, 0:1, cols] = s
        acc[b, 1:2, cols] = c
        acc[b, 2:3, cols] = jnp.sum(d * d, axis=0, keepdims=True)

    @pl.when(b == nblocks - 1)
    def _():
        s, c, r = combine(acc[:, 0, :], acc[:, 1, :], acc[:, 2, :])
        lane = lax.broadcasted_iota(jnp.int32, (1, BS), 1) - 3 * chunk[1]
        row = jnp.where(lane == 0, s, jnp.where(lane == 1, c, jnp.where(lane == 2, r, 0.0)))
        for ref in before:
            row = row + ref[0:1, :]
        stat_ref[...] = jnp.broadcast_to(row, stat_ref.shape)


def run_copies(plan, sems):
    copies = [pltpu.make_async_copy(src, dst, sems.at[i]) for i, (src, dst) in enumerate(plan)]
    for cp in copies:
        cp.start()
    for cp in copies:
        cp.wait()


def first_kernel(pick_ref, own_a, l1_a, r1_a, own_b, l1_b, r1_b, yp, y2, ym, sems):
    plan = []
    for k, arrays in enumerate(((own_a, l1_a, r1_a), (own_b, l1_b, r1_b))):
        for row, (out, step) in enumerate(((yp, 4), (y2, 3), (ym, 4))):
            for i, src in enumerate(arrays):
                plan.append((src.at[pick_ref[12 + row * 5 + i]], out.at[k * step + i]))
        plan.append((arrays[1].at[own_a.shape[0] - 1], yp.at[k * 4 + 3]))
        plan.append((arrays[2].at[0], ym.at[k * 4 + 3]))
    run_copies(plan, sems)


def third_kernel(pick_ref, l2, r2, plus, minus, sems):
    plan = []
    for i in range(6):
        plan.append((l2.at[pick_ref[i]], plus.at[i]))
        plan.append((r2.at[pick_ref[6 + i]], minus.at[i]))
    run_copies(plan, sems)


def second_kernel(pick_ref, l2, r2, quarter, yp, y2, ym, sems):
    plan = []
    part, half = quarter.shape[2], quarter.shape[3] // 2
    for row, out in enumerate((yp, y2, ym)):
        for i, src in enumerate((l2, r2)):
            plan.append((src.at[pick_ref[12 + row * 5 + 3 + i]], out.at[i]))
        for g in range(2):
            for k in range(2):
                plan.append(
                    (
                        quarter.at[g, :, :, pl.ds(k * half, half)],
                        out.at[2, :, pl.ds((2 * g + k) * part, part)],
                    )
                )
    run_copies(plan, sems)


def half_kernel(pick_ref, a3, b3, l2, r2, yp, y2, ym, sems):
    plan = []
    for row, out in enumerate((yp, y2, ym)):
        plan += [(a3.at[row + 1], out.at[0]), (b3.at[row + 1], out.at[1])]
        for i, src in enumerate((l2, r2)):
            plan.append((src.at[pick_ref[12 + row * 5 + 3 + i]], out.at[2 + i]))
    run_copies(plan, sems)


def late_kernel(a3, b3, a4, b4, yp, y2, ym, sems):
    last = (a4.at[1], b4.at[0], b4.at[1])
    plan = []
    for row, out in enumerate((yp, y2, ym)):
        plan += [(a3.at[row + 1], out.at[0]), (b3.at[row + 1], out.at[1]), (last[row], out.at[2])]
    run_copies(plan, sems)


def split_kernel(pick_ref, blocks, p0, p1, p2, p3, sems):
    plan = []
    for i, out in enumerate((p0, p1, p2, p3)):
        rows = pl.ds(pl.multiple_of(pick_ref[29 + i], BS // NY), BS // NY)
        for g in range(2):
            plan.append((blocks.at[:, pick_ref[27 + g], rows], out.at[g]))
    run_copies(plan, sems)


def choose_kernel(at, pick_ref, *refs):
    srcs, out, sems = refs[:-2], refs[-2], refs[-1]
    for g in range(2):
        for k, src in enumerate(srcs):
            @pl.when(pick_ref[at + g] == k)
            def _(src=src, g=g):
                pltpu.make_async_copy(src.at[g], out.at[g], sems.at[g]).start()
    for g in range(2):
        pltpu.make_async_copy(srcs[0].at[g], out.at[g], sems.at[g]).wait()


def total(x):
    return jnp.sum(jnp.sum(x, axis=0, keepdims=True), axis=1, keepdims=True)


def combine(s, c, r):
    s_all = total(s)
    c_all = total(c)
    a = jnp.where(s > 0, c / jnp.where(s > 0, s, 1.0), 0.0)
    a_all = jnp.where(s_all > 0, c_all / jnp.where(s_all > 0, s_all, 1.0), 0.0)
    gap = a - a_all
    return s_all, c_all, total(r + (s * gap) * gap)


def finish_kernel(count, gathered, *refs):
    prods = refs[:CALLS]
    vec_ref, out_ref, coef_ref, ab = refs[CALLS:]
    step = pl.program_id(0)

    @pl.when(step == 0)
    def _():
        table = gathered[...]
        parts = [[table[:, 3 * k + i : 3 * k + i + 1] for i in range(3)] for k in range(CALLS)]
        alpha = sum(total(c) for _, c, _ in parts) * (1.0 / count)
        square = 0.0
        for s, c, r in parts:
            gap = jnp.where(s > 0, c / jnp.where(s > 0, s, 1.0), 0.0) - alpha
            square = square + total(r + (s * gap) * gap)
        beta = jnp.sqrt(square * (1.0 / count) + 1e-06)
        ab[0:1, :] = jnp.broadcast_to(alpha, (1, 128))
        ab[1:2, :] = jnp.broadcast_to(1.0 / beta, (1, 128))
        coef_ref[0] = alpha[0, 0]
        coef_ref[1] = beta[0, 0]

    alpha = ab[0:1, 0:1]
    inv = ab[1:2, 0:1]
    for (first, heads), prod in zip(CHUNKS, prods):
        cols = slice(first * HD, (first + heads) * HD)
        out_ref[:, cols] = (prod[...] - alpha * vec_ref[:, cols]) * inv


def z_shift(d):
    return [(y * NZ + z, y * NZ + (z + d) % NZ) for y in range(NY) for z in range(NZ)]


def y_shift(d):
    return [(y * NZ + z, (y + d) % NY * NZ + z) for y in range(NY) for z in range(NZ)]


def send(x, pairs):
    return lax.ppermute(x, "ctx", pairs)


ANY = pl.BlockSpec(memory_space=pltpu.HBM)


def pack(kernel, picks, arrays, shapes, ncopies):
    scalars = () if picks is None else (picks,)
    return pl.pallas_call(
        kernel,
        out_shape=tuple(jax.ShapeDtypeStruct(shape, jnp.bfloat16) for shape in shapes),
        grid_spec=pltpu.PrefetchScalarGridSpec(
            num_scalar_prefetch=len(scalars),
            grid=(),
            in_specs=[ANY] * len(arrays),
            out_specs=tuple(pl.BlockSpec(memory_space=pltpu.VMEM) for _ in shapes),
            scratch_shapes=[pltpu.SemaphoreType.DMA((ncopies,))],
        ),
        cost_estimate=pl.CostEstimate(flops=0, bytes_accessed=6000000, transcendentals=0),
    )(*scalars, *arrays)


def tables(rand_blocks, global_ids, me, nblocks, nctx):
    my_y, my_z = me // NZ, me % NZ
    requests = rand_blocks.reshape(nctx, nblocks * 3)
    mine = lax.dynamic_index_in_dim(requests, me, 0, keepdims=False)
    pairs = [(i, 1, -2) for i in range(4)] + [(0, 2, -2), (1, 2, -2)]
    pairs += [(i, -1, 2) for i in range(4)] + [(2, -2, 2), (3, -2, 2)]
    for row in (1, 2, 3):
        pairs += [(row, 0, d) for d in (0, -1, 1, -2, 2)]
    offsets = jnp.array(pairs, jnp.int32)
    consumer = ((my_y + offsets[:, 0]) & (NY - 1)) * NZ + ((my_z + offsets[:, 1]) & (NZ - 1))
    source = my_y * NZ + ((my_z + offsets[:, 2]) & (NZ - 1))
    shift = nblocks.bit_length() - 1
    wanted = requests[consumer]
    picks = jnp.sum(
        jnp.where((wanted >> shift) == source[:, None], wanted & (nblocks - 1), 0), axis=1
    )
    g_shard = global_ids >> shift
    g_y, g_z = g_shard >> 3, g_shard & (NZ - 1)
    arange4 = jnp.arange(NY)
    picks = jnp.concatenate(
        [
            picks,
            global_ids & (nblocks - 1),
            ((my_y + arange4) & (NY - 1)) * (BS // NY),
            (my_y - g_y) & (NY - 1),
            (my_z - g_z) & (NZ - 1),
        ]
    ).astype(jnp.int32)
    src = mine >> shift
    inside = mine & (nblocks - 1)
    dy = ((src >> 3) - my_y) & (NY - 1)
    dz = (my_z - src) & (NZ - 1)
    late = (dz >= 3) & (dz <= 5)
    near_slot = jnp.where(late, 0, inside)
    order = jnp.where(
        late, jnp.where(dz == 3, 0, jnp.where(dz == 5, 1, 2)),
        jnp.where(dz == 0, 0, jnp.where(dz == 1, 1, jnp.where(dz == 7, 2, jnp.where(dz == 2, 3, 4)))),
    )
    row = jnp.where(dy == 1, 1, jnp.where(dy == 2, 2, 0))
    second = (dz == 2) | (dz == 6)
    block = jnp.arange(nblocks)
    edges = jnp.stack([me == 0, me == nctx - 1]).astype(jnp.int32)
    piece_rows = ((my_y - arange4) & (NY - 1)) * (BS // NY)
    codes = []
    for chunk in range(2):
        edge_slot = chunk * 4 + 3
        far = jnp.where(late, LYP, jnp.where(second, FP if chunk else MP, YP)) + row
        base = jnp.where(late, 0, jnp.where(second, 2 * chunk - 3, chunk * jnp.where(row == 2, 3, 4)))
        if chunk == 0:
            far = jnp.where(dz == 4, FP + row, far)
            base = jnp.where(dz == 4, -2, base)
        rand_code = jnp.where(dy == 0, dz * 8 + near_slot, far * 8 + order + base).reshape(nblocks, 3)
        left = jnp.where(
            block == 0, jnp.where(my_z == 0, YP * 8 + edge_slot, L1 * 8 + nblocks - 1), block - 1
        )
        right = jnp.where(
            block == nblocks - 1, jnp.where(my_z == NZ - 1, YM * 8 + edge_slot, R1 * 8), block + 1
        )
        listed = jnp.concatenate([jnp.stack([left, block, right], axis=1), rand_code], axis=1)
        codes.append(jnp.concatenate([listed.reshape(-1), edges, piece_rows]).astype(jnp.int32))
    return picks, codes


def whole_step(queries, key_value, lanczos_vec, rand_blocks, global_ids):
    rows, width = queries.shape
    nblocks = rows // BS
    nctx = lax.axis_size("ctx")
    nhead = lax.axis_size("head")
    me = lax.axis_index("ctx")
    picks, codes = tables(rand_blocks, global_ids, me, nblocks, nctx)
    blocks = key_value.reshape(2, nblocks, BS, width)
    piece = (2, 2, BS // NY, width)
    quarters = pack(split_kernel, picks, (blocks,), (piece,) * NY, 8)
    held = (
        quarters[0],
        send(quarters[1], y_shift(1)),
        send(quarters[2], y_shift(2)),
        send(quarters[3], y_shift(-1)),
    )
    (mine,) = pack(functools.partial(choose_kernel, 33), picks, held, (piece,), 2)
    from_left = send(mine, z_shift(1))
    from_right = send(mine, z_shift(-1))
    (close,) = pack(
        functools.partial(choose_kernel, 35), picks,
        (mine, from_left, mine, mine, mine, mine, mine, from_right), (piece,), 2,
    )
    hop_left = send(close, z_shift(3))
    hop_right = send(close, z_shift(-3))
    (quarter,) = pack(
        functools.partial(choose_kernel, 35), picks,
        (close, close, hop_left, hop_left, hop_left, hop_right, hop_right, close), (piece,), 2,
    )
    cw = CHUNKS[0][1] * HD

    def slots(count):
        return (count, 2, BS, cw)

    def rows_of(packed):
        return tuple(send(x, y_shift(d)) for x, d in zip(packed, (1, 2, -1)))

    own, l1, r1, l2, r2 = [], [], [], [], []
    for k, (first, heads) in enumerate(CHUNKS):
        own.append(jnp.swapaxes(blocks[..., first * HD : (first + heads) * HD], 0, 1))
        l1.append(send(own[k], z_shift(1)))
        r1.append(send(own[k], z_shift(-1)))
        l2.append(send(l1[k], z_shift(1)))
        r2.append(send(r1[k], z_shift(-1)))
    y1 = rows_of(
        pack(
            first_kernel, picks, (own[0], l1[0], r1[0], own[1], l1[1], r1[1]),
            (slots(8), slots(6), slots(8)), 22,
        ),
    )
    plus, minus = pack(third_kernel, picks, (l2[0], r2[0]), (slots(6), slots(6)), 12)
    a3, b3 = send(plus, z_shift(1)), send(minus, z_shift(-1))
    y2 = rows_of(pack(second_kernel, picks, (l2[0], r2[0], quarter), (slots(3),) * 3, 18))
    plus, minus = pack(third_kernel, picks, (l2[1], r2[1]), (slots(6), slots(6)), 12)
    c3, d3 = send(plus, z_shift(1)), send(minus, z_shift(-1))
    a4, b4 = send(a3[4:6], z_shift(1)), send(b3[4:6], z_shift(-1))
    c4, d4 = send(c3[4:6], z_shift(1)), send(d3[4:6], z_shift(-1))
    y3a = rows_of(pack(half_kernel, picks, (a3, b3, l2[1], r2[1]), (slots(4),) * 3, 12))
    y4a = rows_of((a4[1:2], b4[0:1], b4[1:2]))
    y3b = rows_of(pack(late_kernel, None, (c3, d3, c4, d4), (slots(3),) * 3, 9))

    def by_code(y):
        return (y[0], y[2], y[1])

    sources = (
        (own[0], l1[0], l2[0], a3, a4, b3, r2[0], r1[0]) + by_code(y1) + by_code(y3a) + by_code(y2)
        + by_code(y4a),
        (own[1], l1[1], l2[1], c3, c4, d3, r2[1], r1[1]) + by_code(y1) + by_code(y3b) + by_code(y2)
        + by_code(y3a),
    )
    products = []
    stats = []
    keys = LIST * BS
    for k, arrays in enumerate(sources):
        stat_rows = 8 if k + 1 < len(sources) else nctx * nhead
        product, stat = pl.pallas_call(
            functools.partial(attention_kernel, nblocks, (CHUNKS[k][0], k), len(arrays)),
            out_shape=(
                jax.ShapeDtypeStruct((rows, cw), jnp.float32),
                jax.ShapeDtypeStruct((stat_rows, BS), jnp.float32),
            ),
            grid_spec=pltpu.PrefetchScalarGridSpec(
                num_scalar_prefetch=1,
                grid=(nblocks,),
                in_specs=[pl.BlockSpec((BS, cw), lambda b, *_, k=k: (b, k))] * 2
                + [ANY] * (len(arrays) + 1)
                + [pl.BlockSpec((8, BS), lambda b, *_: (0, 0))] * len(stats),
                out_specs=(
                    pl.BlockSpec((BS, cw), lambda b, *_: (b, 0)),
                    pl.BlockSpec((stat_rows, BS), lambda b, *_: (0, 0)),
                ),
                scratch_shapes=[
                    pltpu.VMEM((2, 2, keys, cw), jnp.bfloat16),
                    pltpu.SemaphoreType.DMA((2, 2 * LIST)),
                    pltpu.VMEM((nblocks, 8, cw), jnp.float32),
                ],
            ),
            cost_estimate=pl.CostEstimate(
                flops=10 * rows * keys * cw, bytes_accessed=16 * rows * cw,
                transcendentals=rows * keys * (cw // HD),
            ),
        )(codes[k], queries, lanczos_vec, *arrays, quarter, *stats)
        products.append(product)
        stats = [stat]
    gathered = lax.all_to_all(stats[0], ("ctx", "head"), 0, 0, tiled=True)
    count = float(rows * width * nctx * nhead)
    step = rows // 4
    fin_spec = pl.BlockSpec((step, width), lambda i: (i, 0))
    part_specs = [pl.BlockSpec((step, heads * HD), lambda i: (i, 0)) for _, heads in CHUNKS]
    next_vec, coef = pl.pallas_call(
        functools.partial(finish_kernel, count),
        out_shape=(
            jax.ShapeDtypeStruct((rows, width), jnp.float32),
            jax.ShapeDtypeStruct((2,), jnp.float32),
        ),
        grid=(4,),
        in_specs=[pl.BlockSpec((nctx * nhead, 128), lambda i: (0, 0))] + part_specs + [fin_spec],
        out_specs=(fin_spec, pl.BlockSpec(memory_space=pltpu.SMEM)),
        scratch_shapes=[pltpu.VMEM((8, 128), jnp.float32)],
        name="finish",
    )(gathered, *products, lanczos_vec)
    return next_vec, coef


def solution(mesh):
    placed = (P("ctx", "head"), P(None, "ctx", "head"), P("ctx", "head"), P(), P())
    return jax.shard_map(
        whole_step, mesh=mesh, in_specs=placed, out_specs=(P("ctx", "head"), P()), check_vma=False
    )
```
